32 devices in a mesh: groups: 2 (over x), col: 16 (over z, y, core).
Axes of the slice: x: 2, y: 2, z: 4, core: 2. Of those that a mesh axis runs over, the one named last changes fastest.
Arguments:
- trajectory: float32 [2048, 64], P('groups'), parts along dimension 0, may hold values from -6 to 6
- offsets: int32 [4], P('groups'), parts along dimension 0, may hold values from 0 to 896
- landmarks: float32 [16384, 64], replicated, may hold values from -6 to 6
- landmark_ids: int32 [16384], replicated, may hold values from 0 to 16383, each once
- inv_width: float32 [16384], replicated, may hold values from 0.25 to 2
- lower_pairs: float32 [6, 4096, 4096], P(None, 'col'), may hold values from -0.046875 to 0.046875
- diag_inverse: float32 [4, 4096, 4096], P(None, None, 'col')
Outputs:
- whitened: float32 [4, 4096, 512], P(None, 'col', 'groups'), parts along dimension 2
The draws below stay inside these ranges and needn't reach their ends.
There are 2 independent parts, one for each index of `groups`. The reference program is written for one: setup_inputs(seed, part) draws one part's arguments, and reference() takes and returns one part's arrays. A program takes and returns all parts, laid end to end along the dimension named above; an argument that names none is the same for every part. Nothing has to cross between parts.
All inputs are finite; a program needn't handle non-finite values.
Results may differ from the reference program's by a relative error of at most 0.0001.
Values sent between devices are 32-bit elements; how exact they have to be, the bound alone decides.
No kernel may reach another device: no remote copies, remote signals or barrier semaphores. Data moves between devices by JAX's collectives and lax.ppermute only.
A program may use at most 128 MiB of HBM per device.

```python
import math
import jax
import jax.numpy as jnp
from jax import lax

F = 64
SEC = 4096
NSEC = 4
BATCH = 128
NMB = 2
M = 16384
NPAIR = 6
TRAJ = 1024


def draw_diag_inverse(key, part):
    key_off = jax.random.fold_in(key, 11)
    key_diag = jax.random.fold_in(key, 23)
    offdiag = jax.random.normal(key_off, (NSEC, SEC, SEC), jnp.float32)
    diagonal = jax.random.uniform(key_diag, (NSEC, SEC), jnp.float32, 0.5, 1.5)
    offdiag = offdiag / jnp.sqrt(jnp.float32(SEC))
    index = jnp.arange(SEC)
    below = (index[:, None] > index[None, :])[None, :, :]
    identity = (index[:, None] == index[None, :]).astype(jnp.float32)[None, :, :]
    return jnp.where(below, offdiag, 0.0) + diagonal[:, :, None] * identity


def shard_levels(stream_key, shape, split, smallest, largest):
    def one(axis_at, parts):
        steps = jax.random.uniform(jax.random.fold_in(jax.random.fold_in(stream_key, 6), axis_at), (parts,), jnp.float32, smallest / len(split), largest / len(split))
        return jnp.repeat(jnp.exp(steps), shape[axis_at] // parts).reshape((-1,) + (1,) * (len(shape) - axis_at - 1))

    loudness = one(*split[0])
    for cut in split[1:]:
        loudness = loudness * one(*cut)
    return loudness


def scatter_about(stream_key, extent, width, limit, shards=(), held_as=jnp.bfloat16):
    factor_of = shard_levels(stream_key, extent, shards, -0.22, 0.18) if shards else 1.0
    array = jax.random.normal(stream_key, extent, jnp.float32) * width * factor_of
    return jnp.minimum(jnp.maximum(array, -limit), limit).astype(held_as)


def setup_inputs(seed: int = 0, part: int = 0) -> dict:
    splits = jax.random.split(jax.random.key(seed), 8)
    part_splits = jax.random.split(jax.random.fold_in(splits[7], part), 8)
    trajectory = scatter_about(part_splits[0], (TRAJ, F), 1.0, 6.0, (), jnp.float32)
    offsets = jax.random.randint(part_splits[1], (NMB,), 0, TRAJ - BATCH + 1).astype(jnp.int32)
    landmarks = scatter_about(splits[2], (M, F), 1.0, 6.0, (), jnp.float32)
    landmark_ids = jax.random.permutation(splits[3], M).astype(jnp.int32)
    inv_width = jnp.clip(jnp.exp(jax.random.uniform(splits[4], (M,), jnp.float32, math.log(0.25), math.log(2.0))), 0.25, 2.0)
    lower_pairs = scatter_about(splits[5], (NPAIR, SEC, SEC), M ** -0.5, 0.046875, ((1, 16),), jnp.float32)
    diag_inverse = draw_diag_inverse(jax.random.fold_in(splits[7], 71), part)
    return dict(trajectory=trajectory, offsets=offsets, landmarks=landmarks, landmark_ids=landmark_ids, inv_width=inv_width, lower_pairs=lower_pairs, diag_inverse=diag_inverse)


def reference(trajectory, offsets, landmarks, landmark_ids, inv_width, lower_pairs, diag_inverse):
    snapshots = jnp.concatenate([lax.dynamic_slice_in_dim(trajectory, offsets[m].astype(jnp.int32), BATCH, 0) for m in range(NMB)], axis=0)
    centers = jnp.take(landmarks, landmark_ids, axis=0)
    rates = jnp.take(inv_width, landmark_ids)
    cross = jnp.dot(centers, snapshots.T, precision=lax.Precision.HIGHEST, preferred_element_type=jnp.float32)
    dist = jnp.sum(snapshots * snapshots, axis=1)[None, :] + jnp.sum(centers * centers, axis=1)[:, None] - 2.0 * cross
    kernel = jnp.exp(-rates[:, None] * dist / F).reshape(NSEC, SEC, NMB * BATCH)
    solved = []
    for sec_idx in range(NSEC):
        pending = kernel[sec_idx]
        for prior in range(sec_idx):
            pair = sec_idx * (sec_idx - 1) // 2 + prior
            pending = pending - jnp.dot(lower_pairs[pair], solved[prior], precision=lax.Precision.HIGHEST, preferred_element_type=jnp.float32)
        solved.append(jnp.dot(diag_inverse[sec_idx], pending, precision=lax.Precision.HIGHEST, preferred_element_type=jnp.float32))
    return jnp.stack(solved, axis=0)
```

```python
import functools

import jax
import jax.numpy as jnp
from jax import lax
from jax.experimental import pallas as pl
from jax.experimental.pallas import tpu as pltpu
from jax.sharding import PartitionSpec as P

BATCH = 128
COL = "col"


def layout_of(mesh):
    axis = mesh.axis_names.index(COL)
    devices = mesh.devices
    line = devices.swapaxes(0, axis).reshape(devices.shape[axis], -1)[:, 0]
    count = len(line)
    cores = 1
    if count % 2 == 0 and getattr(line[0], "coords", 0) == getattr(line[1], "coords", 0):
        cores = 2
    chips = [line[i] for i in range(0, count, cores)]
    inner = 1
    if hasattr(chips[0], "coords") and len(chips) > 1:
        start = list(chips[0].coords)
        step = [a != b for a, b in zip(start, chips[1].coords)]
        inner = 1
        while inner < len(chips) and all(
            moved or a == b for moved, a, b in zip(step, start, chips[inner].coords)
        ):
            inner += 1
        if len(chips) % inner:
            inner = 1
    outer = len(chips) // inner
    if outer == 1:
        outer, inner = inner, 1
    return outer, inner, cores


class Grid:
    def __init__(self, extents):
        self.extents = extents
        self.count = extents[0] * extents[1] * extents[2]

    def split(self, index):
        outer, inner, core = self.extents
        return index // (inner * core), (index // core) % inner, index % core

    def join(self, z, y, c):
        outer, inner, core = self.extents
        return (z * inner + y) * core + c

    def shift(self, dz, dy, dc):
        pairs = []
        for index in range(self.count):
            z, y, c = self.split(index)
            pairs.append((index, self.join(*self.moved((z, y, c), (dz, dy, dc)))))
        return pairs

    def moved(self, place, by):
        out = []
        for at, step, size in zip(place, by, self.extents):
            power = size & (size - 1) == 0
            out.append(at ^ step if power else (at + step) % size)
        return tuple(out)

    def back(self, place, by):
        out = []
        for at, step, size in zip(place, by, self.extents):
            power = size & (size - 1) == 0
            out.append(at ^ step if power else (at - step) % size)
        return tuple(out)

    def send(self, value, dz=0, dy=0, dc=0):
        return lax.ppermute(value, COL, self.shift(dz, dy, dc))


def halves(value):
    high = value.astype(jnp.bfloat16)
    low = (value - high.astype(jnp.float32)).astype(jnp.bfloat16)
    return high, low


def three_pass(left, right):
    width = right.shape[1]
    left_high, left_low = halves(left)
    right_high, right_low = halves(right)
    both = jnp.concatenate([right_high, right_low], axis=1)
    main = jnp.dot(left_high, both, preferred_element_type=jnp.float32)
    rest = jnp.dot(left_low, right_high, preferred_element_type=jnp.float32)
    return main[:, :width] + (main[:, width:] + rest)


def diag_kernel(sec_idx, blocks, order_ref, diag_ref, x_ref, *refs):
    outs, (buf, sems) = refs[:-2], refs[-2:]
    owned = buf.shape[1]
    copies = []
    for at in range(blocks):
        rows = pl.ds(pl.multiple_of(order_ref[at] * owned, owned), owned)
        copies.append(pltpu.make_async_copy(diag_ref.at[sec_idx, rows, :], buf.at[at], sems.at[at]))
        copies[-1].start()
    x = x_ref[...]
    for at in range(blocks):
        copies[at].wait()
        per = blocks // len(outs)
        outs[at // per][pl.ds((at % per) * owned, owned), :] = three_pass(buf[at], x)


def diag_product(diag_inverse, x, sec_idx, order, parts):
    blocks = order.shape[0]
    owned = x.shape[0]
    width = x.shape[1]
    shape = jax.ShapeDtypeStruct((blocks // parts * owned, width), jnp.float32)
    return pl.pallas_call(
        functools.partial(diag_kernel, sec_idx, blocks),
        out_shape=[shape] * parts,
        in_specs=[
            pl.BlockSpec(memory_space=pltpu.SMEM),
            pl.BlockSpec(memory_space=pl.ANY),
            pl.BlockSpec(memory_space=pltpu.VMEM),
        ],
        out_specs=[pl.BlockSpec(memory_space=pltpu.VMEM)] * parts,
        scratch_shapes=[
            pltpu.VMEM((blocks, owned, owned), jnp.float32),
            pltpu.SemaphoreType.DMA((blocks,)),
        ],
        name=f"diag{sec_idx}",
    )(order, diag_inverse, x)


def pair_kernel(pair, count, order_ref, lower_ref, pending_ref, *refs):
    pieces, (out_ref, buf, sems) = refs[:count], refs[count:]
    owned = out_ref.shape[0]
    blocks = buf.shape[0]
    copies = []
    for at in range(blocks):
        cols = pl.ds(pl.multiple_of(order_ref[at] * owned, owned), owned)
        copies.append(pltpu.make_async_copy(lower_ref.at[pair, :, cols], buf.at[at], sems.at[at]))
        copies[-1].start()
    total = pending_ref[...]
    at = 0
    for piece in pieces:
        for part in range(piece.shape[0] // owned):
            copies[at].wait()
            total = total - three_pass(buf[at], piece[pl.ds(part * owned, owned), :])
            at += 1
    out_ref[...] = total


def pair_product(lower_pairs, pending, pieces, pair, order):
    blocks = order.shape[0]
    owned = pending.shape[0]
    return pl.pallas_call(
        functools.partial(pair_kernel, pair, len(pieces)),
        out_shape=jax.ShapeDtypeStruct(pending.shape, jnp.float32),
        in_specs=[
            pl.BlockSpec(memory_space=pltpu.SMEM),
            pl.BlockSpec(memory_space=pl.ANY),
            pl.BlockSpec(memory_space=pltpu.VMEM),
        ]
        + [pl.BlockSpec(memory_space=pltpu.VMEM)] * len(pieces),
        out_specs=pl.BlockSpec(memory_space=pltpu.VMEM),
        scratch_shapes=[
            pltpu.VMEM((blocks, owned, owned), jnp.float32),
            pltpu.SemaphoreType.DMA((blocks,)),
        ],
        name=f"pair{pair}",
    )(order, lower_pairs, pending, *pieces)


def body(grid, trajectory, offsets, landmarks, landmark_ids, inv_width, lower_pairs, diag_inverse):
    nsec = diag_inverse.shape[0]
    sec = diag_inverse.shape[1]
    owned = diag_inverse.shape[2]
    features = landmarks.shape[1]
    outer, inner, cores = grid.extents
    me = lax.axis_index(COL)
    place = grid.split(me)
    first = me * owned

    def places(dc, toward):
        step = grid.moved if toward else grid.back
        inners = reversed(range(inner)) if toward else range(inner)
        return jnp.stack(
            [grid.join(*step(place, (dz, dy, dc))) for dy in inners for dz in range(outer)]
        ).astype(jnp.int32)

    to_core = [places(dc, True) for dc in range(cores)]
    from_core = [places(dc, False) for dc in range(cores)]

    own_ids = lax.dynamic_slice_in_dim(landmark_ids.reshape(nsec, sec), first, owned, 1).reshape(-1)
    centers = jnp.take(landmarks, own_ids, axis=0)
    rates = jnp.take(inv_width, own_ids)
    center_sq = jnp.sum(centers * centers, axis=1)[:, None]
    pending = []
    for m in range(offsets.shape[0]):
        snap = lax.dynamic_slice_in_dim(trajectory, offsets[m], BATCH, 0)
        cross = jnp.dot(centers, snap.T, precision=lax.Precision.HIGHEST, preferred_element_type=jnp.float32)
        dist = jnp.sum(snap * snap, axis=1)[None, :] + center_sq - 2.0 * cross
        kernel = jnp.exp(-rates[:, None] * dist / features)
        pending.append([kernel[s * owned : (s + 1) * owned] for s in range(nsec)])

    def reduce_scatter(x, sec_idx):
        cut = lambda arr, i: arr[i * owned : (i + 1) * owned]
        parts = diag_product(diag_inverse, x, sec_idx, to_core[-1], inner)
        if cores > 1:
            got = [grid.send(part, dc=cores - 1) for part in parts]
            own = diag_product(diag_inverse, x, sec_idx, to_core[0], inner)
            parts = [a + b for a, b in zip(own, got)]
        mine = parts[-1]
        for at, dy in enumerate(reversed(range(1, inner))):
            mine = mine + grid.send(parts[at], dy=dy)
        total = cut(mine, 0)
        got = [grid.send(cut(mine, dz), dz=dz) for dz in range(1, outer)]
        for one in got:
            total = total + one
        return total

    def all_gather(mine):
        column = [mine] + [grid.send(mine, dz=dz) for dz in range(1, outer)]
        column = jnp.concatenate(column, axis=0)
        plane = [column] + [grid.send(column, dy=dy) for dy in range(1, inner)]
        return [[grid.send(one, dc=dc) if dc else one for one in plane] for dc in range(cores)]

    chunks = len(pending)
    results = [[None] * nsec for _ in range(chunks)]
    for sec_idx in range(nsec):
        for m in range(chunks):
            mine = reduce_scatter(pending[m][sec_idx], sec_idx)
            results[m][sec_idx] = mine
            if sec_idx + 1 == nsec:
                continue
            pieces = all_gather(mine)
            for later in range(sec_idx + 1, nsec):
                pair = later * (later - 1) // 2 + sec_idx
                for dc in range(cores):
                    pending[m][later] = pair_product(lower_pairs, pending[m][later], pieces[dc], pair, from_core[dc])
    return jnp.concatenate([jnp.stack(one, axis=0) for one in results], axis=2)


def solution(mesh):
    grid = Grid(layout_of(mesh))
    in_specs = (
        P("groups", None),
        P("groups"),
        P(),
        P(),
        P(),
        P(None, COL, None),
        P(None, None, COL),
    )
    out_specs = P(None, COL, "groups")
    return jax.shard_map(
        functools.partial(body, grid), mesh=mesh, in_specs=in_specs, out_specs=out_specs, check_vma=False
    )
```

```python
import functools

import jax
import jax.numpy as jnp
from jax import lax
from jax.experimental import pallas as pl
from jax.experimental.pallas import tpu as pltpu
from jax.sharding import PartitionSpec as P

BATCH = 128
COL = "col"


def layout_of(mesh):
    axis = mesh.axis_names.index(COL)
    devices = mesh.devices
    line = devices.swapaxes(0, axis).reshape(devices.shape[axis], -1)[:, 0]
    count = len(line)
    cores = 1
    if count % 2 == 0 and getattr(line[0], "coords", 0) == getattr(line[1], "coords", 0):
        cores = 2
    chips = [line[i] for i in range(0, count, cores)]
    inner = 1
    if hasattr(chips[0], "coords") and len(chips) > 1:
        start = list(chips[0].coords)
        step = [a != b for a, b in zip(start, chips[1].coords)]
        inner = 1
        while inner < len(chips) and all(
            moved or a == b for moved, a, b in zip(step, start, chips[inner].coords)
        ):
            inner += 1
        if len(chips) % inner:
            inner = 1
    outer = len(chips) // inner
    if outer == 1:
        outer, inner = inner, 1
    return outer, inner, cores


class Grid:
    def __init__(self, extents):
        self.extents = extents
        self.count = extents[0] * extents[1] * extents[2]

    def split(self, index):
        outer, inner, core = self.extents
        return index // (inner * core), (index // core) % inner, index % core

    def join(self, z, y, c):
        outer, inner, core = self.extents
        return (z * inner + y) * core + c

    def shift(self, dz, dy, dc):
        pairs = []
        for index in range(self.count):
            z, y, c = self.split(index)
            pairs.append((index, self.join(*self.moved((z, y, c), (dz, dy, dc)))))
        return pairs

    def moved(self, place, by):
        out = []
        for at, step, size in zip(place, by, self.extents):
            power = size & (size - 1) == 0
            out.append(at ^ step if power else (at + step) % size)
        return tuple(out)

    def back(self, place, by):
        out = []
        for at, step, size in zip(place, by, self.extents):
            power = size & (size - 1) == 0
            out.append(at ^ step if power else (at - step) % size)
        return tuple(out)

    def send(self, value, dz=0, dy=0, dc=0):
        return lax.ppermute(value, COL, self.shift(dz, dy, dc))


def halves(value):
    high = value.astype(jnp.bfloat16)
    low = (value - high.astype(jnp.float32)).astype(jnp.bfloat16)
    return high, low


def three_pass(left, right):
    width = right.shape[1]
    left_high, left_low = halves(left)
    right_high, right_low = halves(right)
    both = jnp.concatenate([right_high, right_low], axis=1)
    main = jnp.dot(left_high, both, preferred_element_type=jnp.float32)
    rest = jnp.dot(left_low, right_high, preferred_element_type=jnp.float32)
    return main[:, :width] + (main[:, width:] + rest)


def lower_part(meta_ref, lower_ref, pair, pending, pieces, owned, bufs):
    lbuf, wbuf, lsem, wsem, stage = bufs
    outer, _, zrows = lbuf.shape
    subs = len(pieces)
    from_z, from_sub = outer, 2 * outer + subs

    def l_copy(k):
        cols = pl.ds(pl.multiple_of(meta_ref[from_z + k] * zrows, zrows), zrows)
        return pltpu.make_async_copy(lower_ref.at[pair, :, cols], lbuf.at[k], lsem.at[k])

    def w_copy(sub, k):
        rows = pl.ds(pl.multiple_of(meta_ref[from_sub + sub] * owned, owned), owned)
        return pltpu.make_async_copy(
            pieces[sub].at[pl.ds(k * owned, owned), :], wbuf.at[k, rows, :], wsem.at[k * subs + sub]
        )

    for k in range(outer):
        if stage != "lower":
            for sub in range(subs):
                w_copy(sub, k).start()
        l_copy(k).start()

    def finish(total):
        def step(k, carry):
            if stage != "lower":
                for sub in range(subs):
                    w_copy(sub, k).wait()
            l_copy(k).wait()
            return carry - three_pass(lbuf[k], wbuf[k])

        return lax.fori_loop(0, outer, step, total)

    return finish


def section_kernel(sec_idx, pair, subs, meta_ref, diag_ref, lower_ref, pending_ref, *refs):
    pieces = refs[:subs] if pair is not None else ()
    refs = refs[len(pieces) :]
    outs, refs = refs[:subs], refs[subs:]
    dbuf, obuf, xbuf, dsem, osem, xsem = refs[:6]
    outer, zrows, owned = dbuf.shape
    to_sub = 2 * outer
    x_copy = pltpu.make_async_copy(pending_ref, xbuf, xsem)
    x_copy.start()
    finish = None
    if pair is not None:
        lbuf, wbuf, lsem, wsem = refs[6:]
        finish = lower_part(meta_ref, lower_ref, pair, None, pieces, owned, (lbuf, wbuf, lsem, wsem, "all"))

    def d_copy(k):
        rows = pl.ds(pl.multiple_of(meta_ref[k] * zrows, zrows), zrows)
        return pltpu.make_async_copy(diag_ref.at[sec_idx, rows, :], dbuf.at[k], dsem.at[k])

    def o_copy(sub, k):
        rows = pl.ds(pl.multiple_of(k * owned, owned), owned)
        return pltpu.make_async_copy(obuf.at[sub, rows, :], outs[sub].at[rows, :], osem.at[k * subs + sub])

    for k in range(outer):
        d_copy(k).start()
    x_copy.wait()
    x = xbuf[...]
    if finish is not None:
        x = finish(x)
    width = x.shape[1]
    x_high, x_low = halves(x)
    both = jnp.concatenate([x_high, x_low], axis=1)

    def step(k, carry):
        d_copy(k).wait()
        for sub in range(subs):
            rows = pl.ds(pl.multiple_of(meta_ref[to_sub + sub] * owned, owned), owned)
            high, low = halves(dbuf[k, rows, :])
            main = jnp.dot(high, both, preferred_element_type=jnp.float32)
            rest = jnp.dot(low, x_high, preferred_element_type=jnp.float32)
            at = pl.ds(pl.multiple_of(k * owned, owned), owned)
            obuf[sub, at, :] = main[:, :width] + (main[:, width:] + rest)
            o_copy(sub, k).start()
        return carry

    lax.fori_loop(0, outer, step, 0)
    for k in range(outer):
        for sub in range(subs):
            o_copy(sub, k).wait()


def section_product(grid, meta, diag_inverse, lower_pairs, pending, pieces, sec_idx, pair):
    outer, inner, cores = grid.extents
    subs = inner * cores
    owned, width = pending.shape
    zrows = subs * owned
    dma = pltpu.SemaphoreType.DMA
    scratch = [
        pltpu.VMEM((outer, zrows, owned), jnp.float32),
        pltpu.VMEM((subs, outer * owned, width), jnp.float32),
        pltpu.VMEM((owned, width), jnp.float32),
        dma((outer,)),
        dma((outer * subs,)),
        dma(()),
    ]
    if pair is not None:
        scratch += [
            pltpu.VMEM((outer, owned, zrows), jnp.float32),
            pltpu.VMEM((outer, zrows, width), jnp.float32),
            dma((outer,)),
            dma((outer * subs,)),
        ]
    anywhere = pl.BlockSpec(memory_space=pl.ANY)
    return pl.pallas_call(
        functools.partial(section_kernel, sec_idx, pair, subs),
        out_shape=[jax.ShapeDtypeStruct((outer * owned, width), jnp.float32)] * subs,
        in_specs=[pl.BlockSpec(memory_space=pltpu.SMEM)] + [anywhere] * (3 + len(pieces)),
        out_specs=[anywhere] * subs,
        scratch_shapes=scratch,
        name=f"section{sec_idx}",
    )(meta, diag_inverse, lower_pairs, pending, *pieces)


def older_kernel(pairs, subs, meta_ref, lower_ref, *refs):
    count = len(pairs)
    pendings, refs = refs[:count], refs[count:]
    pieces, refs = refs[:subs], refs[subs:]
    outs, refs = refs[:count], refs[count:]
    wbuf, wsem = refs[:2]
    bufs, sems = refs[2 : 2 + count], refs[2 + count :]
    finishers = []
    for at, pair in enumerate(pairs):
        stage = "all" if at == 0 else "lower"
        finishers.append(
            lower_part(
                meta_ref, lower_ref, pair, None, pieces, outs[at].shape[0], (bufs[at], wbuf, sems[at], wsem, stage)
            )
        )
    for at in range(count):
        outs[at][...] = finishers[at](pendings[at][...])


def older_product(grid, meta, lower_pairs, pendings, pieces, pairs):
    outer, inner, cores = grid.extents
    subs = inner * cores
    owned, width = pendings[0].shape
    zrows = subs * owned
    dma = pltpu.SemaphoreType.DMA
    anywhere = pl.BlockSpec(memory_space=pl.ANY)
    vmem = pl.BlockSpec(memory_space=pltpu.VMEM)
    count = len(pairs)
    return pl.pallas_call(
        functools.partial(older_kernel, pairs, subs),
        out_shape=[jax.ShapeDtypeStruct((owned, width), jnp.float32)] * count,
        in_specs=[pl.BlockSpec(memory_space=pltpu.SMEM), anywhere] + [vmem] * count + [anywhere] * subs,
        out_specs=[vmem] * count,
        scratch_shapes=[pltpu.VMEM((outer, zrows, width), jnp.float32), dma((outer * subs,))]
        + [pltpu.VMEM((outer, owned, zrows), jnp.float32)] * count
        + [dma((outer,))] * count,
        name="older",
    )(meta, lower_pairs, *pendings, *pieces)


def body(grid, trajectory, offsets, landmarks, landmark_ids, inv_width, lower_pairs, diag_inverse):
    nsec = diag_inverse.shape[0]
    sec = diag_inverse.shape[1]
    owned = diag_inverse.shape[2]
    features = landmarks.shape[1]
    outer, inner, cores = grid.extents
    me = lax.axis_index(COL)
    place = grid.split(me)
    first = me * owned

    def coordinates(step):
        zs = [step(place, (dz, 0, 0))[0] for dz in range(outer)]
        subs = []
        for dc in range(cores):
            for dy in range(inner):
                _, y, c = step(place, (0, dy, dc))
                subs.append(y * cores + c)
        return zs, subs

    to_z, to_sub = coordinates(grid.moved)
    from_z, from_sub = coordinates(grid.back)
    meta = jnp.stack(to_z + from_z + to_sub + from_sub).astype(jnp.int32)

    own_ids = lax.dynamic_slice_in_dim(landmark_ids.reshape(nsec, sec), first, owned, 1).reshape(-1)
    centers = jnp.take(landmarks, own_ids, axis=0)
    rates = jnp.take(inv_width, own_ids)
    center_sq = jnp.sum(centers * centers, axis=1)[:, None]
    pending = []
    for m in range(offsets.shape[0]):
        snap = lax.dynamic_slice_in_dim(trajectory, offsets[m], BATCH, 0)
        cross = jnp.dot(centers, snap.T, precision=lax.Precision.HIGHEST, preferred_element_type=jnp.float32)
        dist = jnp.sum(snap * snap, axis=1)[None, :] + center_sq - 2.0 * cross
        kernel = jnp.exp(-rates[:, None] * dist / features)
        pending.append([kernel[s * owned : (s + 1) * owned] for s in range(nsec)])

    def reduce_scatter(parts):
        cut = lambda arr, i: arr[i * owned : (i + 1) * owned]
        rows = [parts[dc * inner : (dc + 1) * inner] for dc in range(cores)]
        plane = []
        for dy in reversed(range(inner)):
            total = rows[0][dy]
            for dc in range(1, cores):
                total = total + grid.send(rows[dc][dy], dc=dc)
            plane.append(total)
        mine = plane[-1]
        for at, dy in enumerate(reversed(range(1, inner))):
            mine = mine + grid.send(plane[at], dy=dy)
        total = cut(mine, 0)
        got = [grid.send(cut(mine, dz), dz=dz) for dz in range(1, outer)]
        for one in got:
            total = total + one
        return total

    def all_gather(mine):
        column = [mine] + [grid.send(mine, dz=dz) for dz in range(1, outer)]
        column = jnp.concatenate(column, axis=0)
        plane = [column] + [grid.send(column, dy=dy) for dy in range(1, inner)]
        out = []
        for dc in range(cores):
            out += [grid.send(one, dc=dc) if dc else one for one in plane]
        return out

    chunks = len(pending)
    results = [[None] * nsec for _ in range(chunks)]
    pieces = [()] * chunks
    for sec_idx in range(nsec):
        newest = sec_idx * (sec_idx - 1) // 2 + sec_idx - 1 if sec_idx else None
        for m in range(chunks):
            parts = section_product(
                grid, meta, diag_inverse, lower_pairs, pending[m][sec_idx], pieces[m], sec_idx, newest
            )
            later = range(sec_idx + 1, nsec)
            if sec_idx and len(later):
                pairs = [s * (s - 1) // 2 + sec_idx - 1 for s in later]
                done = older_product(grid, meta, lower_pairs, [pending[m][s] for s in later], pieces[m], pairs)
                for s, one in zip(later, done):
                    pending[m][s] = one
            results[m][sec_idx] = reduce_scatter(parts)
            if sec_idx + 1 < nsec:
                pieces[m] = all_gather(results[m][sec_idx])
    return jnp.concatenate([jnp.stack(one, axis=0) for one in results], axis=2)


def solution(mesh):
    grid = Grid(layout_of(mesh))
    in_specs = (
        P("groups", None),
        P("groups"),
        P(),
        P(),
        P(),
        P(None, COL, None),
        P(None, None, COL),
    )
    out_specs = P(None, COL, "groups")
    return jax.shard_map(
        functools.partial(body, grid), mesh=mesh, in_specs=in_specs, out_specs=out_specs, check_vma=False
    )
```

```python
import functools

import jax
import jax.numpy as jnp
from jax import lax
from jax.experimental import pallas as pl
from jax.experimental.pallas import tpu as pltpu
from jax.sharding import PartitionSpec as P


BATCH = 128
COL = "col"


def layout_of(mesh):
    axis = mesh.axis_names.index(COL)
    devices = mesh.devices
    line = devices.swapaxes(0, axis).reshape(devices.shape[axis], -1)[:, 0]
    count = len(line)
    cores = 1
    if count % 2 == 0 and getattr(line[0], "coords", 0) == getattr(line[1], "coords", 0):
        cores = 2
    chips = [line[i] for i in range(0, count, cores)]
    inner = 1
    if hasattr(chips[0], "coords") and len(chips) > 1:
        start = list(chips[0].coords)
        step = [a != b for a, b in zip(start, chips[1].coords)]
        inner = 1
        while inner < len(chips) and all(
            moved or a == b for moved, a, b in zip(step, start, chips[inner].coords)
        ):
            inner += 1
        if len(chips) % inner:
            inner = 1
    outer = len(chips) // inner
    if outer == 1:
        outer, inner = inner, 1
    return outer, inner, cores


class Grid:
    def __init__(self, extents):
        self.extents = extents
        self.count = extents[0] * extents[1] * extents[2]

    def split(self, index):
        _, inner, core = self.extents
        return index // (inner * core), (index // core) % inner, index % core

    def join(self, z, y, c):
        _, inner, core = self.extents
        return (z * inner + y) * core + c

    def shift(self, dz, dy, dc):
        pairs = []
        for index in range(self.count):
            z, y, c = self.split(index)
            pairs.append((index, self.join(*self.moved((z, y, c), (dz, dy, dc)))))
        return pairs

    def moved(self, place, by):
        out = []
        for at, step, size in zip(place, by, self.extents):
            power = size & (size - 1) == 0
            out.append(at ^ step if power else (at + step) % size)
        return tuple(out)

    def back(self, place, by):
        out = []
        for at, step, size in zip(place, by, self.extents):
            power = size & (size - 1) == 0
            out.append(at ^ step if power else (at - step) % size)
        return tuple(out)

    def send(self, value, dz=0, dy=0, dc=0):
        return lax.ppermute(value, COL, self.shift(dz, dy, dc))


def halves(value):
    high = value.astype(jnp.bfloat16)
    low = (value - high.astype(jnp.float32)).astype(jnp.bfloat16)
    return high, low


def three_pass(left, right):
    width = right.shape[1]
    left_high, left_low = halves(left)
    right_high, right_low = halves(right)
    both = jnp.concatenate([right_high, right_low], axis=1)
    main = jnp.dot(left_high, both, preferred_element_type=jnp.float32)
    rest = jnp.dot(left_low, right_high, preferred_element_type=jnp.float32)
    return main[:, :width] + (main[:, width:] + rest)


def lower_part(meta_ref, lower_ref, pair, pieces, owned, bufs):
    lbuf, wbuf, lsem, wsem, stage = bufs
    outer, _, zrows = lbuf.shape
    chunks, subs = len(pieces), len(pieces[0])
    width = wbuf.shape[2] // chunks
    from_z, from_sub = outer, 2 * outer + subs

    def l_copy(k):
        cols = pl.ds(pl.multiple_of(meta_ref[from_z + k] * zrows, zrows), zrows)
        return pltpu.make_async_copy(lower_ref.at[pair, :, cols], lbuf.at[k], lsem.at[k])

    def w_copy(m, sub, k):
        rows = pl.ds(pl.multiple_of(meta_ref[from_sub + sub] * owned, owned), owned)
        return pltpu.make_async_copy(
            pieces[m][sub].at[pl.ds(k * owned, owned), :],
            wbuf.at[k, rows, pl.ds(m * width, width)],
            wsem.at[(k * subs + sub) * chunks + m],
        )

    for k in range(outer):
        if stage != "lower":
            for sub in range(subs):
                for m in range(chunks):
                    w_copy(m, sub, k).start()
        l_copy(k).start()

    def finish(total):
        def step(k, carry):
            if stage != "lower":
                for sub in range(subs):
                    for m in range(chunks):
                        w_copy(m, sub, k).wait()
            l_copy(k).wait()
            return carry - three_pass(lbuf[k], wbuf[k])

        return lax.fori_loop(0, outer, step, total)

    return finish


def section_kernel(sec_idx, pair, subs, meta_ref, diag_ref, lower_ref, pending_ref, *refs):
    pieces = refs[:subs] if pair is not None else ()
    refs = refs[len(pieces) :]
    outs, refs = refs[:subs], refs[subs:]
    dbuf, obuf, xbuf, dsem, osem, xsem = refs[:6]
    outer, zrows, owned = dbuf.shape
    to_sub = 2 * outer
    x_copy = pltpu.make_async_copy(pending_ref, xbuf, xsem)
    x_copy.start()
    finish = None
    if pair is not None:
        lbuf, wbuf, lsem, wsem = refs[6:]
        finish = lower_part(meta_ref, lower_ref, pair, [pieces], owned, (lbuf, wbuf, lsem, wsem, "all"))

    def d_copy(k):
        rows = pl.ds(pl.multiple_of(meta_ref[k] * zrows, zrows), zrows)
        return pltpu.make_async_copy(diag_ref.at[sec_idx, rows, :], dbuf.at[k], dsem.at[k])

    def o_copy(sub, k):
        rows = pl.ds(pl.multiple_of(k * owned, owned), owned)
        return pltpu.make_async_copy(obuf.at[sub, rows, :], outs[sub].at[rows, :], osem.at[k * subs + sub])

    for k in range(outer):
        d_copy(k).start()
    x_copy.wait()
    x = xbuf[...]
    if finish is not None:
        x = finish(x)
    width = x.shape[1]
    x_high, x_low = halves(x)
    both = jnp.concatenate([x_high, x_low], axis=1)

    def step(k, carry):
        d_copy(k).wait()
        for sub in range(subs):
            rows = pl.ds(pl.multiple_of(meta_ref[to_sub + sub] * owned, owned), owned)
            high, low = halves(dbuf[k, rows, :])
            main = jnp.dot(high, both, preferred_element_type=jnp.float32)
            rest = jnp.dot(low, x_high, preferred_element_type=jnp.float32)
            at = pl.ds(pl.multiple_of(k * owned, owned), owned)
            obuf[sub, at, :] = main[:, :width] + (main[:, width:] + rest)
            o_copy(sub, k).start()
        return carry

    lax.fori_loop(0, outer, step, 0)
    for k in range(outer):
        for sub in range(subs):
            o_copy(sub, k).wait()


def section_product(grid, meta, diag_inverse, lower_pairs, pending, pieces, sec_idx, pair):
    outer, inner, cores = grid.extents
    subs = inner * cores
    owned, width = pending.shape
    zrows = subs * owned
    dma = pltpu.SemaphoreType.DMA
    scratch = [
        pltpu.VMEM((outer, zrows, owned), jnp.float32),
        pltpu.VMEM((subs, outer * owned, width), jnp.float32),
        pltpu.VMEM((owned, width), jnp.float32),
        dma((outer,)),
        dma((outer * subs,)),
        dma(()),
    ]
    if pair is not None:
        scratch += [
            pltpu.VMEM((outer, owned, zrows), jnp.float32),
            pltpu.VMEM((outer, zrows, width), jnp.float32),
            dma((outer,)),
            dma((outer * subs,)),
        ]
    anywhere = pl.BlockSpec(memory_space=pl.ANY)
    return pl.pallas_call(
        functools.partial(section_kernel, sec_idx, pair, subs),
        out_shape=[jax.ShapeDtypeStruct((outer * owned, width), jnp.float32)] * subs,
        in_specs=[pl.BlockSpec(memory_space=pltpu.SMEM)] + [anywhere] * (3 + len(pieces)),
        out_specs=[anywhere] * subs,
        scratch_shapes=scratch,
    )(meta, diag_inverse, lower_pairs, pending, *pieces)


def older_kernel(pairs, subs, chunks, meta_ref, lower_ref, *refs):
    count = len(pairs)
    pendings, refs = refs[: count * chunks], refs[count * chunks :]
    pieces = [refs[m * subs : (m + 1) * subs] for m in range(chunks)]
    refs = refs[chunks * subs :]
    outs, refs = refs[: count * chunks], refs[count * chunks :]
    wbuf, wsem = refs[:2]
    bufs, sems = refs[2 : 2 + count], refs[2 + count :]
    owned, width = outs[0].shape
    finishers = []
    for at, pair in enumerate(pairs):
        bound = (bufs[at], wbuf, sems[at], wsem, "all" if at == 0 else "lower")
        finishers.append(lower_part(meta_ref, lower_ref, pair, pieces, owned, bound))
    for at in range(count):
        mine = pendings[at * chunks : (at + 1) * chunks]
        total = finishers[at](jnp.concatenate([one[...] for one in mine], axis=1))
        for m in range(chunks):
            outs[at * chunks + m][...] = total[:, m * width : (m + 1) * width]


def older_product(grid, meta, lower_pairs, pendings, pieces, pairs):
    outer, inner, cores = grid.extents
    subs, chunks = inner * cores, len(pieces)
    owned, width = pendings[0][0].shape
    zrows = subs * owned
    dma = pltpu.SemaphoreType.DMA
    anywhere = pl.BlockSpec(memory_space=pl.ANY)
    vmem = pl.BlockSpec(memory_space=pltpu.VMEM)
    count = len(pairs)
    out = pl.pallas_call(
        functools.partial(older_kernel, pairs, subs, chunks),
        out_shape=[jax.ShapeDtypeStruct((owned, width), jnp.float32)] * (count * chunks),
        in_specs=[pl.BlockSpec(memory_space=pltpu.SMEM), anywhere]
        + [vmem] * (count * chunks)
        + [anywhere] * (subs * chunks),
        out_specs=[vmem] * (count * chunks),
        scratch_shapes=[pltpu.VMEM((outer, zrows, width * chunks), jnp.float32), dma((outer * subs * chunks,))]
        + [pltpu.VMEM((outer, owned, zrows), jnp.float32)] * count
        + [dma((outer,))] * count,
        name="older",
    )(meta, lower_pairs, *[one for row in pendings for one in row], *[one for row in pieces for one in row])
    return [out[at * chunks : (at + 1) * chunks] for at in range(count)]


def body(grid, trajectory, offsets, landmarks, landmark_ids, inv_width, lower_pairs, diag_inverse):
    nsec = diag_inverse.shape[0]
    sec = diag_inverse.shape[1]
    owned = diag_inverse.shape[2]
    features = landmarks.shape[1]
    outer, inner, cores = grid.extents
    me = lax.axis_index(COL)
    place = grid.split(me)
    first = me * owned

    def coordinates(step):
        zs = [step(place, (dz, 0, 0))[0] for dz in range(outer)]
        subs = []
        for dc in range(cores):
            for dy in range(inner):
                _, y, c = step(place, (0, dy, dc))
                subs.append(y * cores + c)
        return zs, subs

    to_z, to_sub = coordinates(grid.moved)
    from_z, from_sub = coordinates(grid.back)
    meta = jnp.stack(to_z + from_z + to_sub + from_sub).astype(jnp.int32)

    own_ids = lax.dynamic_slice_in_dim(landmark_ids.reshape(nsec, sec), first, owned, 1).reshape(-1)
    centers = jnp.take(landmarks, own_ids, axis=0)
    rates = jnp.take(inv_width, own_ids)
    center_sq = jnp.sum(centers * centers, axis=1)[:, None]
    chunks = offsets.shape[0]
    pending = []
    for m in range(chunks):
        snap = lax.dynamic_slice_in_dim(trajectory, offsets[m], BATCH, 0)
        cross = jnp.dot(centers, snap.T, precision=lax.Precision.HIGHEST, preferred_element_type=jnp.float32)
        dist = jnp.sum(snap * snap, axis=1)[None, :] + center_sq - 2.0 * cross
        kernel = jnp.exp(-rates[:, None] * dist / features)
        pending.append([kernel[s * owned : (s + 1) * owned] for s in range(nsec)])

    cut = lambda arr, i: arr[i * owned : (i + 1) * owned]

    def chunk_steps(m):
        pieces = ()
        for sec_idx in range(nsec):
            newest = sec_idx * (sec_idx - 1) // 2 + sec_idx - 1 if sec_idx else None
            yield
            parts = section_product(grid, meta, diag_inverse, lower_pairs, pending[m][sec_idx], pieces, sec_idx, newest)
            newest_pieces[m] = pieces
            own, rest = parts[:inner], parts[inner:]
            got = [
                [grid.send(rest[(dc - 1) * inner + dy], dc=dc) for dc in range(1, cores)]
                for dy in reversed(range(inner))
            ]
            yield
            plane = []
            for dy in range(1, inner):
                total = own[dy]
                for one in got[inner - 1 - dy]:
                    total = total + one
                plane.append(grid.send(total, dy=dy))
            yield
            mine = own[0]
            for one in got[-1] + plane:
                mine = mine + one
            got = [grid.send(cut(mine, dz), dz=dz) for dz in range(1, outer)]
            yield
            mine = cut(mine, 0)
            for one in got:
                mine = mine + one
            results[m][sec_idx] = mine
            if sec_idx + 1 == nsec:
                return
            got = [grid.send(mine, dz=dz) for dz in range(1, outer)]
            yield
            column = jnp.concatenate([mine] + got, axis=0)
            plane = [column] + [grid.send(column, dy=dy) for dy in range(1, inner)]
            across = [[grid.send(column, dc=dc)] for dc in range(1, cores)]
            yield
            for dc in range(1, cores):
                across[dc - 1] += [grid.send(one, dc=dc) for one in plane[1:]]
            pieces = tuple(plane + [one for row in across for one in row])

    def older_steps():
        for sec_idx in range(1, nsec - 1):
            later = range(sec_idx + 1, nsec)
            pairs = [s * (s - 1) // 2 + sec_idx - 1 for s in later]
            rows = [[pending[m][s] for m in range(chunks)] for s in later]
            done = older_product(grid, meta, lower_pairs, rows, newest_pieces, pairs)
            for s, row in zip(later, done):
                for m in range(chunks):
                    pending[m][s] = row[m]
            yield

    results = [[None] * nsec for _ in range(chunks)]
    newest_pieces = [None] * chunks
    steps = [chunk_steps(m) for m in range(chunks)] + [older_steps()]
    for one in steps[:chunks]:
        next(one)
    for who, _, _ in step_order(nsec, chunks):
        next(steps[who], None)
    return jnp.concatenate([jnp.stack(one, axis=0) for one in results], axis=2)


STEPS = 6


def step_order(nsec, chunks):
    keyed = []
    for sec_idx in range(nsec):
        for step in range(STEPS if sec_idx + 1 < nsec else STEPS - 2):
            at = sec_idx * STEPS + step
            lag = 0.5 if 0 < at < 5 else 1.5
            keyed += [(at + m * lag, at, (m, sec_idx, step)) for m in range(chunks)]
        if 0 < sec_idx < nsec - 1:
            at = sec_idx * STEPS + 1
            keyed.append((at + 1.5 * (chunks - 1), at + 1, (chunks, sec_idx, 0)))
    return [entry for _, _, entry in sorted(keyed)]


def solution(mesh):
    grid = Grid(layout_of(mesh))
    in_specs = (
        P("groups", None),
        P("groups"),
        P(),
        P(),
        P(),
        P(None, COL, None),
        P(None, None, COL),
    )
    out_specs = P(None, COL, "groups")
    step = jax.shard_map(
        functools.partial(body, grid), mesh=mesh, in_specs=in_specs, out_specs=out_specs, check_vma=False
    )

    def whole(trajectory, offsets, *rest):
        run = step
        return run(trajectory, offsets, *rest)

    return whole
```

```python
import functools

import jax
import jax.numpy as jnp
from jax import lax
from jax.experimental import pallas as pl
from jax.experimental.pallas import tpu as pltpu
from jax.sharding import PartitionSpec as P


BATCH = 128
COL = "col"


def layout_of(mesh):
    axis = mesh.axis_names.index(COL)
    devices = mesh.devices
    line = devices.swapaxes(0, axis).reshape(devices.shape[axis], -1)[:, 0]
    count = len(line)
    cores = 1
    if count % 2 == 0 and getattr(line[0], "coords", 0) == getattr(line[1], "coords", 0):
        cores = 2
    chips = [line[i] for i in range(0, count, cores)]
    inner = 1
    if hasattr(chips[0], "coords") and len(chips) > 1:
        start = list(chips[0].coords)
        step = [a != b for a, b in zip(start, chips[1].coords)]
        inner = 1
        while inner < len(chips) and all(
            moved or a == b for moved, a, b in zip(step, start, chips[inner].coords)
        ):
            inner += 1
        if len(chips) % inner:
            inner = 1
    outer = len(chips) // inner
    if outer == 1:
        outer, inner = inner, 1
    return outer, inner, cores


class Grid:
    def __init__(self, extents):
        self.extents = extents
        self.count = extents[0] * extents[1] * extents[2]

    def split(self, index):
        _, inner, core = self.extents
        return index // (inner * core), (index // core) % inner, index % core

    def join(self, z, y, c):
        _, inner, core = self.extents
        return (z * inner + y) * core + c

    def shift(self, dz, dy, dc):
        pairs = []
        for index in range(self.count):
            z, y, c = self.split(index)
            pairs.append((index, self.join(*self.moved((z, y, c), (dz, dy, dc)))))
        return pairs

    def moved(self, place, by):
        out = []
        for at, step, size in zip(place, by, self.extents):
            power = size & (size - 1) == 0
            out.append(at ^ step if power else (at + step) % size)
        return tuple(out)

    def back(self, place, by):
        out = []
        for at, step, size in zip(place, by, self.extents):
            power = size & (size - 1) == 0
            out.append(at ^ step if power else (at - step) % size)
        return tuple(out)

    def send(self, value, dz=0, dy=0, dc=0):
        return lax.ppermute(value, COL, self.shift(dz, dy, dc))


def halves(value):
    high = value.astype(jnp.bfloat16)
    low = (value - high.astype(jnp.float32)).astype(jnp.bfloat16)
    return high, low


def three_pass(left, right):
    width = right.shape[1]
    left_high, left_low = halves(left)
    right_high, right_low = halves(right)
    both = jnp.concatenate([right_high, right_low], axis=1)
    main = jnp.dot(left_high, both, preferred_element_type=jnp.float32)
    rest = jnp.dot(left_low, right_high, preferred_element_type=jnp.float32)
    return main[:, :width] + (main[:, width:] + rest)


def lower_part(meta_ref, lower_ref, pair, pieces, owned, bufs):
    lbuf, wbuf, lsem, wsem, stage = bufs
    outer, _, zrows = lbuf.shape
    chunks, subs = len(pieces), len(pieces[0])
    width = wbuf.shape[2] // chunks
    from_z, from_sub = outer, 2 * outer + subs

    def l_copy(k):
        cols = pl.ds(pl.multiple_of(meta_ref[from_z + k] * zrows, zrows), zrows)
        return pltpu.make_async_copy(lower_ref.at[pair, :, cols], lbuf.at[k], lsem.at[k])

    def w_copy(m, sub, k):
        rows = pl.ds(pl.multiple_of(meta_ref[from_sub + sub] * owned, owned), owned)
        return pltpu.make_async_copy(
            pieces[m][sub].at[pl.ds(k * owned, owned), :],
            wbuf.at[k, rows, pl.ds(m * width, width)],
            wsem.at[(k * subs + sub) * chunks + m],
        )

    for k in range(outer):
        if stage != "lower":
            for sub in range(subs):
                for m in range(chunks):
                    w_copy(m, sub, k).start()
        l_copy(k).start()

    def finish(total):
        def step(k, carry):
            if stage != "lower":
                for sub in range(subs):
                    for m in range(chunks):
                        w_copy(m, sub, k).wait()
            l_copy(k).wait()
            return carry - three_pass(lbuf[k], wbuf[k])

        return lax.fori_loop(0, outer, step, total)

    return finish


def section_kernel(sec_idx, pair, subs, meta_ref, diag_ref, lower_ref, pending_ref, *refs):
    pieces = refs[:subs] if pair is not None else ()
    refs = refs[len(pieces) :]
    outs, refs = refs[:subs], refs[subs:]
    dbuf, obuf, xbuf, dsem, osem, xsem = refs[:6]
    outer, zrows, owned = dbuf.shape
    to_sub = 2 * outer
    x_copy = pltpu.make_async_copy(pending_ref, xbuf, xsem)
    x_copy.start()
    finish = None
    if pair is not None:
        lbuf, wbuf, lsem, wsem = refs[6:]
        finish = lower_part(meta_ref, lower_ref, pair, [pieces], owned, (lbuf, wbuf, lsem, wsem, "all"))

    def d_copy(k):
        rows = pl.ds(pl.multiple_of(meta_ref[k] * zrows, zrows), zrows)
        return pltpu.make_async_copy(diag_ref.at[sec_idx, rows, :], dbuf.at[k], dsem.at[k])

    def o_copy(sub, k):
        rows = pl.ds(pl.multiple_of(k * owned, owned), owned)
        return pltpu.make_async_copy(obuf.at[sub, rows, :], outs[sub].at[rows, :], osem.at[k * subs + sub])

    for k in range(outer):
        d_copy(k).start()
    x_copy.wait()
    x = xbuf[...]
    if finish is not None:
        x = finish(x)
    width = x.shape[1]
    x_high, x_low = halves(x)
    both = jnp.concatenate([x_high, x_low], axis=1)

    def step(k, carry):
        d_copy(k).wait()
        for sub in range(subs):
            rows = pl.ds(pl.multiple_of(meta_ref[to_sub + sub] * owned, owned), owned)
            high, low = halves(dbuf[k, rows, :])
            main = jnp.dot(high, both, preferred_element_type=jnp.float32)
            rest = jnp.dot(low, x_high, preferred_element_type=jnp.float32)
            at = pl.ds(pl.multiple_of(k * owned, owned), owned)
            obuf[sub, at, :] = main[:, :width] + (main[:, width:] + rest)
            o_copy(sub, k).start()
        return carry

    lax.fori_loop(0, outer, step, 0)
    for k in range(outer):
        for sub in range(subs):
            o_copy(sub, k).wait()


def section_product(grid, meta, diag_inverse, lower_pairs, pending, pieces, sec_idx, pair):
    outer, inner, cores = grid.extents
    subs = inner * cores
    owned, width = pending.shape
    zrows = subs * owned
    dma = pltpu.SemaphoreType.DMA
    scratch = [
        pltpu.VMEM((outer, zrows, owned), jnp.float32),
        pltpu.VMEM((subs, outer * owned, width), jnp.float32),
        pltpu.VMEM((owned, width), jnp.float32),
        dma((outer,)),
        dma((outer * subs,)),
        dma(()),
    ]
    if pair is not None:
        scratch += [
            pltpu.VMEM((outer, owned, zrows), jnp.float32),
            pltpu.VMEM((outer, zrows, width), jnp.float32),
            dma((outer,)),
            dma((outer * subs,)),
        ]
    anywhere = pl.BlockSpec(memory_space=pl.ANY)
    return pl.pallas_call(
        functools.partial(section_kernel, sec_idx, pair, subs),
        out_shape=[jax.ShapeDtypeStruct((outer * owned, width), jnp.float32)] * subs,
        in_specs=[pl.BlockSpec(memory_space=pltpu.SMEM)] + [anywhere] * (3 + len(pieces)),
        out_specs=[anywhere] * subs,
        scratch_shapes=scratch,
    )(meta, diag_inverse, lower_pairs, pending, *pieces)


def feature_kernel(sections, sec, meta_ref, offsets_ref, ids_ref, table_ref, width_ref, path_ref, *outs):
    features = table_ref.shape[0]
    owned, lanes = outs[0].shape
    first = meta_ref[meta_ref.shape[0] - 1]
    chunks = offsets_ref.shape[0]
    lane = lax.broadcasted_iota(jnp.int32, (features, lanes), 1)
    one_lane = lax.broadcasted_iota(jnp.int32, (1, lanes), 1)
    last = path_ref.shape[1] // lanes - 1
    snaps = []
    for m in range(chunks):
        block = jnp.minimum(offsets_ref[m] // lanes, last)
        inside = offsets_ref[m] - block * lanes
        here = path_ref[:, pl.ds(pl.multiple_of(block * lanes, lanes), lanes)]
        after = path_ref[:, pl.ds(pl.multiple_of(jnp.minimum(block + 1, last) * lanes, lanes), lanes)]
        turn = (lanes - inside) % lanes
        snap = jnp.where(lane < lanes - inside, pltpu.roll(here, turn, 1), pltpu.roll(after, turn, 1))
        snaps.append((snap, jnp.sum(snap * snap, axis=0, keepdims=True)))
    for at, sec_idx in enumerate(sections):
        for group in range(owned // lanes):
            base = sec_idx * sec + first + group * lanes

            def pick(i, carry):
                centers, rates = carry
                number = ids_ref[base + i]
                block = number // lanes
                turn = (i - number % lanes + lanes) % lanes
                column = table_ref[:, pl.ds(pl.multiple_of(block * lanes, lanes), lanes)]
                centers = jnp.where(lane == i, pltpu.roll(column, turn, 1), centers)
                rates = jnp.where(one_lane == i, pltpu.roll(width_ref[pl.ds(block, 1), :], turn, 1), rates)
                return centers, rates

            zero = jnp.zeros((features, lanes), jnp.float32)
            centers, rates = lax.fori_loop(0, lanes, pick, (zero, zero[:1]), unroll=8)
            pad = lanes - features
            flat = jnp.concatenate([centers, jnp.broadcast_to(rates, (pad, lanes))], axis=0).T
            centers, rates = flat[:, :features], flat[:, features : features + 1]
            center_sq = jnp.sum(centers * centers, axis=1, keepdims=True)
            for m, (snap, snap_sq) in enumerate(snaps):
                cross = jnp.dot(
                    centers, snap, precision=lax.Precision.HIGHEST, preferred_element_type=jnp.float32
                )
                dist = snap_sq + center_sq - 2.0 * cross
                outs[at * chunks + m][pl.ds(group * lanes, lanes), :] = jnp.exp(-rates * dist / features)


def features_of(meta, offsets, landmark_ids, landmarks, inv_width, trajectory, owned, sec, sections):
    chunks = offsets.shape[0]
    smem = pl.BlockSpec(memory_space=pltpu.SMEM)
    vmem = pl.BlockSpec(memory_space=pltpu.VMEM)
    out = pl.pallas_call(
        functools.partial(feature_kernel, sections, sec),
        out_shape=[jax.ShapeDtypeStruct((owned, BATCH), jnp.float32)] * (chunks * len(sections)),
        in_specs=[smem, smem, smem, vmem, vmem, vmem],
        out_specs=[vmem] * (chunks * len(sections)),
        name="features",
    )(meta, offsets, landmark_ids, landmarks.T, inv_width.reshape(-1, BATCH), trajectory.T)
    return [out[at * chunks : (at + 1) * chunks] for at in range(len(sections))]


def older_kernel(pairs, subs, chunks, meta_ref, lower_ref, *refs):
    count = len(pairs)
    pendings, refs = refs[: count * chunks], refs[count * chunks :]
    pieces = [refs[m * subs : (m + 1) * subs] for m in range(chunks)]
    refs = refs[chunks * subs :]
    outs, refs = refs[: count * chunks], refs[count * chunks :]
    wbuf, wsem = refs[:2]
    bufs, sems = refs[2 : 2 + count], refs[2 + count :]
    owned, width = outs[0].shape
    finishers = []
    for at, pair in enumerate(pairs):
        bound = (bufs[at], wbuf, sems[at], wsem, "all" if at == 0 else "lower")
        finishers.append(lower_part(meta_ref, lower_ref, pair, pieces, owned, bound))
    for at in range(count):
        mine = pendings[at * chunks : (at + 1) * chunks]
        total = finishers[at](jnp.concatenate([one[...] for one in mine], axis=1))
        for m in range(chunks):
            outs[at * chunks + m][...] = total[:, m * width : (m + 1) * width]


def older_product(grid, meta, lower_pairs, pendings, pieces, pairs):
    outer, inner, cores = grid.extents
    subs, chunks = inner * cores, len(pieces)
    owned, width = pendings[0][0].shape
    zrows = subs * owned
    dma = pltpu.SemaphoreType.DMA
    anywhere = pl.BlockSpec(memory_space=pl.ANY)
    vmem = pl.BlockSpec(memory_space=pltpu.VMEM)
    count = len(pairs)
    out = pl.pallas_call(
        functools.partial(older_kernel, pairs, subs, chunks),
        out_shape=[jax.ShapeDtypeStruct((owned, width), jnp.float32)] * (count * chunks),
        in_specs=[pl.BlockSpec(memory_space=pltpu.SMEM), anywhere]
        + [vmem] * (count * chunks)
        + [anywhere] * (subs * chunks),
        out_specs=[vmem] * (count * chunks),
        scratch_shapes=[pltpu.VMEM((outer, zrows, width * chunks), jnp.float32), dma((outer * subs * chunks,))]
        + [pltpu.VMEM((outer, owned, zrows), jnp.float32)] * count
        + [dma((outer,))] * count,
        name="older",
    )(meta, lower_pairs, *[one for row in pendings for one in row], *[one for row in pieces for one in row])
    return [out[at * chunks : (at + 1) * chunks] for at in range(count)]


def body(grid, trajectory, offsets, landmarks, landmark_ids, inv_width, lower_pairs, diag_inverse):
    nsec = diag_inverse.shape[0]
    sec = diag_inverse.shape[1]
    owned = diag_inverse.shape[2]
    outer, inner, cores = grid.extents
    me = lax.axis_index(COL)
    place = grid.split(me)
    first = me * owned

    def coordinates(step):
        zs = [step(place, (dz, 0, 0))[0] for dz in range(outer)]
        subs = []
        for dc in range(cores):
            for dy in range(inner):
                _, y, c = step(place, (0, dy, dc))
                subs.append(y * cores + c)
        return zs, subs

    to_z, to_sub = coordinates(grid.moved)
    from_z, from_sub = coordinates(grid.back)
    meta = jnp.stack(to_z + from_z + to_sub + from_sub + [first]).astype(jnp.int32)

    chunks = offsets.shape[0]

    def features_in(sections):
        return features_of(
            meta, offsets, landmark_ids, landmarks, inv_width, trajectory, owned, sec, tuple(sections)
        )

    begin = features_in([0])[0]
    pending = [[begin[m]] + [None] * (nsec - 1) for m in range(chunks)]

    cut = lambda arr, i: arr[i * owned : (i + 1) * owned]

    def chunk_steps(m):
        pieces = ()
        for sec_idx in range(nsec):
            newest = sec_idx * (sec_idx - 1) // 2 + sec_idx - 1 if sec_idx else None
            yield
            parts = section_product(grid, meta, diag_inverse, lower_pairs, pending[m][sec_idx], pieces, sec_idx, newest)
            newest_pieces[m] = pieces
            own, rest = parts[:inner], parts[inner:]
            got = [
                [grid.send(rest[(dc - 1) * inner + dy], dc=dc) for dc in range(1, cores)]
                for dy in reversed(range(inner))
            ]
            yield
            plane = []
            for dy in range(1, inner):
                total = own[dy]
                for one in got[inner - 1 - dy]:
                    total = total + one
                plane.append(grid.send(total, dy=dy))
            yield
            mine = own[0]
            for one in got[-1] + plane:
                mine = mine + one
            got = [grid.send(cut(mine, dz), dz=dz) for dz in range(1, outer)]
            yield
            mine = cut(mine, 0)
            for one in got:
                mine = mine + one
            results[m][sec_idx] = mine
            if sec_idx + 1 == nsec:
                return
            got = [grid.send(mine, dz=dz) for dz in range(1, outer)]
            yield
            column = jnp.concatenate([mine] + got, axis=0)
            plane = [column] + [grid.send(column, dy=dy) for dy in range(1, inner)]
            across = [[grid.send(column, dc=dc)] for dc in range(1, cores)]
            yield
            for dc in range(1, cores):
                across[dc - 1] += [grid.send(one, dc=dc) for one in plane[1:]]
            pieces = tuple(plane + [one for row in across for one in row])

    def older_steps():
        for sec_idx, row in enumerate(features_in(range(1, nsec)), 1):
            for m in range(chunks):
                pending[m][sec_idx] = row[m]
        yield
        for sec_idx in range(1, nsec - 1):
            later = range(sec_idx + 1, nsec)
            pairs = [s * (s - 1) // 2 + sec_idx - 1 for s in later]
            rows = [[pending[m][s] for m in range(chunks)] for s in later]
            done = older_product(grid, meta, lower_pairs, rows, newest_pieces, pairs)
            for s, row in zip(later, done):
                for m in range(chunks):
                    pending[m][s] = row[m]
            yield

    results = [[None] * nsec for _ in range(chunks)]
    newest_pieces = [None] * chunks
    steps = [chunk_steps(m) for m in range(chunks)] + [older_steps()]
    for one in steps[:chunks]:
        next(one)
    for who, _, _ in step_order(nsec, chunks):
        next(steps[who], None)
    return jnp.concatenate([jnp.stack(one, axis=0) for one in results], axis=2)


STEPS = 6


def step_order(nsec, chunks):
    keyed = []
    for sec_idx in range(nsec):
        for step in range(STEPS if sec_idx + 1 < nsec else STEPS - 2):
            at = sec_idx * STEPS + step
            lag = 0.5 if 0 < at < 5 else 1.5
            keyed += [(at + m * lag, at, (m, sec_idx, step)) for m in range(chunks)]
        if sec_idx < nsec - 1:
            at = sec_idx * STEPS + 1
            keyed.append((at + 1.5 * (chunks - 1), at + 1, (chunks, sec_idx, 0)))
    return [entry for _, _, entry in sorted(keyed)]


def solution(mesh):
    grid = Grid(layout_of(mesh))
    in_specs = (
        P("groups", None),
        P("groups"),
        P(),
        P(),
        P(),
        P(None, COL, None),
        P(None, None, COL),
    )
    out_specs = P(None, COL, "groups")
    step = jax.shard_map(
        functools.partial(body, grid), mesh=mesh, in_specs=in_specs, out_specs=out_specs, check_vma=False
    )

    def whole(trajectory, offsets, *rest):
        run = step
        return run(trajectory, offsets, *rest)

    return whole
```

```python
import functools

import jax
import jax.numpy as jnp
from jax import lax
from jax.experimental import pallas as pl
from jax.experimental.pallas import tpu as pltpu
from jax.sharding import PartitionSpec as P


BATCH = 128
COL = "col"


def layout_of(mesh):
    axis = mesh.axis_names.index(COL)
    devices = mesh.devices
    line = devices.swapaxes(0, axis).reshape(devices.shape[axis], -1)[:, 0]
    count = len(line)
    cores = 1
    if count % 2 == 0 and getattr(line[0], "coords", 0) == getattr(line[1], "coords", 0):
        cores = 2
    chips = [line[i] for i in range(0, count, cores)]
    inner = 1
    if hasattr(chips[0], "coords") and len(chips) > 1:
        start = list(chips[0].coords)
        step = [a != b for a, b in zip(start, chips[1].coords)]
        inner = 1
        while inner < len(chips) and all(
            moved or a == b for moved, a, b in zip(step, start, chips[inner].coords)
        ):
            inner += 1
        if len(chips) % inner:
            inner = 1
    outer = len(chips) // inner
    if outer == 1:
        outer, inner = inner, 1
    return outer, inner, cores


class Grid:
    def __init__(self, extents):
        self.extents = extents
        self.count = extents[0] * extents[1] * extents[2]

    def split(self, index):
        _, inner, core = self.extents
        return index // (inner * core), (index // core) % inner, index % core

    def join(self, z, y, c):
        _, inner, core = self.extents
        return (z * inner + y) * core + c

    def shift(self, dz, dy, dc):
        pairs = []
        for index in range(self.count):
            z, y, c = self.split(index)
            pairs.append((index, self.join(*self.moved((z, y, c), (dz, dy, dc)))))
        return pairs

    def moved(self, place, by):
        out = []
        for at, step, size in zip(place, by, self.extents):
            power = size & (size - 1) == 0
            out.append(at ^ step if power else (at + step) % size)
        return tuple(out)

    def back(self, place, by):
        out = []
        for at, step, size in zip(place, by, self.extents):
            power = size & (size - 1) == 0
            out.append(at ^ step if power else (at - step) % size)
        return tuple(out)

    def send(self, value, dz=0, dy=0, dc=0):
        return lax.ppermute(value, COL, self.shift(dz, dy, dc))


def halves(value):
    high = value.astype(jnp.bfloat16)
    low = (value - high.astype(jnp.float32)).astype(jnp.bfloat16)
    return high, low


def three_pass(left, right):
    width = right.shape[1]
    left_high, left_low = halves(left)
    right_high, right_low = halves(right)
    both = jnp.concatenate([right_high, right_low], axis=1)
    main = jnp.dot(left_high, both, preferred_element_type=jnp.float32)
    rest = jnp.dot(left_low, right_high, preferred_element_type=jnp.float32)
    return main[:, :width] + (main[:, width:] + rest)


def lower_part(meta_ref, lower_ref, pair, pieces, owned, bufs):
    lbuf, wbuf, lsem, wsem, stage = bufs
    outer, _, zrows = lbuf.shape
    chunks, subs = len(pieces), len(pieces[0])
    width = wbuf.shape[2] // chunks
    from_z, from_sub = outer, 2 * outer + subs

    def l_copy(k):
        cols = pl.ds(pl.multiple_of(meta_ref[from_z + k] * zrows, zrows), zrows)
        return pltpu.make_async_copy(lower_ref.at[pair, :, cols], lbuf.at[k], lsem.at[k])

    def w_copy(m, sub, k):
        rows = pl.ds(pl.multiple_of(meta_ref[from_sub + sub] * owned, owned), owned)
        return pltpu.make_async_copy(
            pieces[m][sub].at[pl.ds(k * owned, owned), :],
            wbuf.at[k, rows, pl.ds(m * width, width)],
            wsem.at[(k * subs + sub) * chunks + m],
        )

    for k in range(outer):
        if stage != "lower":
            for sub in range(subs):
                for m in range(chunks):
                    w_copy(m, sub, k).start()
        l_copy(k).start()

    def finish(total):
        def step(k, carry):
            if stage != "lower":
                for sub in range(subs):
                    for m in range(chunks):
                        w_copy(m, sub, k).wait()
            l_copy(k).wait()
            return carry - three_pass(lbuf[k], wbuf[k])

        return lax.fori_loop(0, outer, step, total)

    return finish


def section_kernel(sec_idx, pair, subs, meta_ref, diag_ref, lower_ref, pending_ref, *refs):
    pieces = refs[:subs] if pair is not None else ()
    refs = refs[len(pieces) :]
    outs, refs = refs[:subs], refs[subs:]
    dbuf, obuf, xbuf, dsem, osem, xsem = refs[:6]
    outer, zrows, owned = dbuf.shape
    to_sub = 2 * outer
    x_copy = pltpu.make_async_copy(pending_ref, xbuf, xsem)
    x_copy.start()
    finish = None
    if pair is not None:
        lbuf, wbuf, lsem, wsem = refs[6:]
        finish = lower_part(meta_ref, lower_ref, pair, [pieces], owned, (lbuf, wbuf, lsem, wsem, "all"))

    def d_copy(k):
        rows = pl.ds(pl.multiple_of(meta_ref[k] * zrows, zrows), zrows)
        return pltpu.make_async_copy(diag_ref.at[sec_idx, rows, :], dbuf.at[k], dsem.at[k])

    def o_copy(sub, k):
        rows = pl.ds(pl.multiple_of(k * owned, owned), owned)
        return pltpu.make_async_copy(obuf.at[sub, rows, :], outs[sub].at[rows, :], osem.at[k * subs + sub])

    for k in range(outer):
        d_copy(k).start()
    x_copy.wait()
    x = xbuf[...]
    if finish is not None:
        x = finish(x)
    width = x.shape[1]
    x_high, x_low = halves(x)
    both = jnp.concatenate([x_high, x_low], axis=1)

    def step(k, carry):
        d_copy(k).wait()
        for sub in range(subs):
            rows = pl.ds(pl.multiple_of(meta_ref[to_sub + sub] * owned, owned), owned)
            high, low = halves(dbuf[k, rows, :])
            main = jnp.dot(high, both, preferred_element_type=jnp.float32)
            rest = jnp.dot(low, x_high, preferred_element_type=jnp.float32)
            at = pl.ds(pl.multiple_of(k * owned, owned), owned)
            obuf[sub, at, :] = main[:, :width] + (main[:, width:] + rest)
            o_copy(sub, k).start()
        return carry

    lax.fori_loop(0, outer, step, 0)
    for k in range(outer):
        for sub in range(subs):
            o_copy(sub, k).wait()


def section_product(grid, meta, diag_inverse, lower_pairs, pending, pieces, sec_idx, pair):
    outer, inner, cores = grid.extents
    subs = inner * cores
    owned, width = pending.shape
    zrows = subs * owned
    dma = pltpu.SemaphoreType.DMA
    scratch = [
        pltpu.VMEM((outer, zrows, owned), jnp.float32),
        pltpu.VMEM((subs, outer * owned, width), jnp.float32),
        pltpu.VMEM((owned, width), jnp.float32),
        dma((outer,)),
        dma((outer * subs,)),
        dma(()),
    ]
    if pair is not None:
        scratch += [
            pltpu.VMEM((outer, owned, zrows), jnp.float32),
            pltpu.VMEM((outer, zrows, width), jnp.float32),
            dma((outer,)),
            dma((outer * subs,)),
        ]
    anywhere = pl.BlockSpec(memory_space=pl.ANY)
    return pl.pallas_call(
        functools.partial(section_kernel, sec_idx, pair, subs),
        out_shape=[jax.ShapeDtypeStruct((outer * owned, width), jnp.float32)] * subs,
        in_specs=[pl.BlockSpec(memory_space=pltpu.SMEM)] + [anywhere] * (3 + len(pieces)),
        out_specs=[anywhere] * subs,
        scratch_shapes=scratch,
    )(meta, diag_inverse, lower_pairs, pending, *pieces)


def feature_kernel(sections, sec, meta_ref, offsets_ref, ids_ref, table_ref, width_ref, path_ref, *outs):
    features = table_ref.shape[0]
    owned, lanes = outs[0].shape
    first = meta_ref[meta_ref.shape[0] - 1]
    chunks = offsets_ref.shape[0]
    lane = lax.broadcasted_iota(jnp.int32, (features, lanes), 1)
    one_lane = lax.broadcasted_iota(jnp.int32, (1, lanes), 1)
    last = path_ref.shape[1] // lanes - 1
    snaps = []
    for m in range(chunks):
        block = jnp.minimum(offsets_ref[m] // lanes, last)
        inside = offsets_ref[m] - block * lanes
        here = path_ref[:, pl.ds(pl.multiple_of(block * lanes, lanes), lanes)]
        after = path_ref[:, pl.ds(pl.multiple_of(jnp.minimum(block + 1, last) * lanes, lanes), lanes)]
        turn = (lanes - inside) % lanes
        snap = jnp.where(lane < lanes - inside, pltpu.roll(here, turn, 1), pltpu.roll(after, turn, 1))
        snaps.append((snap, jnp.sum(snap * snap, axis=0, keepdims=True)))
    for at, sec_idx in enumerate(sections):
        for group in range(owned // lanes):
            base = sec_idx * sec + first + group * lanes

            def pick(i, carry):
                centers, rates = carry
                number = ids_ref[base + i]
                block = lax.shift_right_logical(number, lanes.bit_length() - 1)
                turn = (i - number) & (lanes - 1)
                column = table_ref[:, pl.ds(pl.multiple_of(block * lanes, lanes), lanes)]
                centers = jnp.where(lane == i, pltpu.roll(column, turn, 1), centers)
                rates = jnp.where(one_lane == i, pltpu.roll(width_ref[pl.ds(block, 1), :], turn, 1), rates)
                return centers, rates

            zero = jnp.zeros((features, lanes), jnp.float32)
            centers, rates = lax.fori_loop(0, lanes, pick, (zero, zero[:1]), unroll=16)
            pad = lanes - features
            flat = jnp.concatenate([centers, jnp.broadcast_to(rates, (pad, lanes))], axis=0).T
            centers, rates = flat[:, :features], flat[:, features : features + 1]
            center_sq = jnp.sum(centers * centers, axis=1, keepdims=True)
            for m, (snap, snap_sq) in enumerate(snaps):
                cross = jnp.dot(
                    centers, snap, precision=lax.Precision.HIGHEST, preferred_element_type=jnp.float32
                )
                dist = snap_sq + center_sq - 2.0 * cross
                outs[at * chunks + m][pl.ds(group * lanes, lanes), :] = jnp.exp(-rates * dist / features)


def features_of(meta, offsets, landmark_ids, landmarks, inv_width, trajectory, owned, sec, sections):
    chunks = offsets.shape[0]
    smem = pl.BlockSpec(memory_space=pltpu.SMEM)
    vmem = pl.BlockSpec(memory_space=pltpu.VMEM)
    out = pl.pallas_call(
        functools.partial(feature_kernel, sections, sec),
        out_shape=[jax.ShapeDtypeStruct((owned, BATCH), jnp.float32)] * (chunks * len(sections)),
        in_specs=[smem, smem, smem, vmem, vmem, vmem],
        out_specs=[vmem] * (chunks * len(sections)),
        name="features",
    )(meta, offsets, landmark_ids, landmarks.T, inv_width.reshape(-1, BATCH), trajectory.T)
    return [out[at * chunks : (at + 1) * chunks] for at in range(len(sections))]


def older_kernel(pairs, subs, chunks, meta_ref, lower_ref, *refs):
    count = len(pairs)
    pendings, refs = refs[: count * chunks], refs[count * chunks :]
    pieces = [refs[m * subs : (m + 1) * subs] for m in range(chunks)]
    refs = refs[chunks * subs :]
    outs, refs = refs[: count * chunks], refs[count * chunks :]
    wbuf, wsem = refs[:2]
    bufs, sems = refs[2 : 2 + count], refs[2 + count :]
    owned, width = outs[0].shape
    finishers = []
    for at, pair in enumerate(pairs):
        bound = (bufs[at], wbuf, sems[at], wsem, "all" if at == 0 else "lower")
        finishers.append(lower_part(meta_ref, lower_ref, pair, pieces, owned, bound))
    for at in range(count):
        mine = pendings[at * chunks : (at + 1) * chunks]
        total = finishers[at](jnp.concatenate([one[...] for one in mine], axis=1))
        for m in range(chunks):
            outs[at * chunks + m][...] = total[:, m * width : (m + 1) * width]


def older_product(grid, meta, lower_pairs, pendings, pieces, pairs):
    outer, inner, cores = grid.extents
    subs, chunks = inner * cores, len(pieces)
    owned, width = pendings[0][0].shape
    zrows = subs * owned
    dma = pltpu.SemaphoreType.DMA
    anywhere = pl.BlockSpec(memory_space=pl.ANY)
    vmem = pl.BlockSpec(memory_space=pltpu.VMEM)
    count = len(pairs)
    out = pl.pallas_call(
        functools.partial(older_kernel, pairs, subs, chunks),
        out_shape=[jax.ShapeDtypeStruct((owned, width), jnp.float32)] * (count * chunks),
        in_specs=[pl.BlockSpec(memory_space=pltpu.SMEM), anywhere]
        + [vmem] * (count * chunks)
        + [anywhere] * (subs * chunks),
        out_specs=[vmem] * (count * chunks),
        scratch_shapes=[pltpu.VMEM((outer, zrows, width * chunks), jnp.float32), dma((outer * subs * chunks,))]
        + [pltpu.VMEM((outer, owned, zrows), jnp.float32)] * count
        + [dma((outer,))] * count,
        name="older",
    )(meta, lower_pairs, *[one for row in pendings for one in row], *[one for row in pieces for one in row])
    return [out[at * chunks : (at + 1) * chunks] for at in range(count)]


def body(grid, trajectory, offsets, landmarks, landmark_ids, inv_width, lower_pairs, diag_inverse):
    nsec = diag_inverse.shape[0]
    sec = diag_inverse.shape[1]
    owned = diag_inverse.shape[2]
    outer, inner, cores = grid.extents
    me = lax.axis_index(COL)
    place = grid.split(me)
    first = me * owned

    def coordinates(step):
        zs = [step(place, (dz, 0, 0))[0] for dz in range(outer)]
        subs = []
        for dc in range(cores):
            for dy in range(inner):
                _, y, c = step(place, (0, dy, dc))
                subs.append(y * cores + c)
        return zs, subs

    to_z, to_sub = coordinates(grid.moved)
    from_z, from_sub = coordinates(grid.back)
    meta = jnp.stack(to_z + from_z + to_sub + from_sub + [first]).astype(jnp.int32)

    chunks = offsets.shape[0]

    def features_in(sections):
        return features_of(
            meta, offsets, landmark_ids, landmarks, inv_width, trajectory, owned, sec, tuple(sections)
        )

    begin = features_in([0])[0]
    pending = [[begin[m]] + [None] * (nsec - 1) for m in range(chunks)]

    cut = lambda arr, i: arr[i * owned : (i + 1) * owned]

    def chunk_steps(m):
        pieces = ()
        for sec_idx in range(nsec):
            newest = sec_idx * (sec_idx - 1) // 2 + sec_idx - 1 if sec_idx else None
            yield
            parts = section_product(grid, meta, diag_inverse, lower_pairs, pending[m][sec_idx], pieces, sec_idx, newest)
            newest_pieces[m] = pieces
            own, rest = parts[:inner], parts[inner:]
            got = [
                [grid.send(rest[(dc - 1) * inner + dy], dc=dc) for dc in range(1, cores)]
                for dy in reversed(range(inner))
            ]
            yield
            plane = []
            for dy in range(1, inner):
                total = own[dy]
                for one in got[inner - 1 - dy]:
                    total = total + one
                plane.append(grid.send(total, dy=dy))
            yield
            mine = own[0]
            for one in got[-1] + plane:
                mine = mine + one
            got = [grid.send(cut(mine, dz), dz=dz) for dz in range(1, outer)]
            yield
            mine = cut(mine, 0)
            for one in got:
                mine = mine + one
            results[m][sec_idx] = mine
            if sec_idx + 1 == nsec:
                return
            got = [grid.send(mine, dz=dz) for dz in range(1, outer)]
            yield
            column = jnp.concatenate([mine] + got, axis=0)
            plane = [column] + [grid.send(column, dy=dy) for dy in range(1, inner)]
            across = [[grid.send(column, dc=dc)] for dc in range(1, cores)]
            yield
            for dc in range(1, cores):
                across[dc - 1] += [grid.send(one, dc=dc) for one in plane[1:]]
            pieces = tuple(plane + [one for row in across for one in row])

    def older_steps():
        for sections in feature_parts(nsec):
            for sec_idx, row in zip(sections, features_in(sections)):
                for m in range(chunks):
                    pending[m][sec_idx] = row[m]
            yield
        for sec_idx in range(1, nsec - 1):
            later = range(sec_idx + 1, nsec)
            pairs = [s * (s - 1) // 2 + sec_idx - 1 for s in later]
            rows = [[pending[m][s] for m in range(chunks)] for s in later]
            done = older_product(grid, meta, lower_pairs, rows, newest_pieces, pairs)
            for s, row in zip(later, done):
                for m in range(chunks):
                    pending[m][s] = row[m]
            yield

    results = [[None] * nsec for _ in range(chunks)]
    newest_pieces = [None] * chunks
    steps = [chunk_steps(m) for m in range(chunks)] + [older_steps()]
    for one in steps[:chunks]:
        next(one)
    for who, _, _ in step_order(nsec, chunks):
        next(steps[who], None)
    return jnp.concatenate([jnp.stack(one, axis=0) for one in results], axis=2)


STEPS = 6


def step_order(nsec, chunks):
    keyed = []
    for sec_idx in range(nsec):
        for step in range(STEPS if sec_idx + 1 < nsec else STEPS - 2):
            at = sec_idx * STEPS + step
            lag = 0.5 if 0 < at < 5 else 1.5
            keyed += [(at + m * lag, at, (m, sec_idx, step)) for m in range(chunks)]
        if sec_idx == 0:
            for part, at in zip(range(len(feature_parts(nsec))), (3.6, 4.6)):
                keyed.append((at, at, (chunks, 0, part)))
        elif sec_idx < nsec - 1:
            at = sec_idx * STEPS + 1
            keyed.append((at + 1.5 * (chunks - 1), at + 1, (chunks, sec_idx, 0)))
    return [entry for _, _, entry in sorted(keyed)]


def feature_parts(nsec):
    return [one for one in (list(range(1, min(2, nsec))), list(range(2, nsec))) if one]


def solution(mesh):
    grid = Grid(layout_of(mesh))
    in_specs = (
        P("groups", None),
        P("groups"),
        P(),
        P(),
        P(),
        P(None, COL, None),
        P(None, None, COL),
    )
    out_specs = P(None, COL, "groups")
    step = jax.shard_map(
        functools.partial(body, grid), mesh=mesh, in_specs=in_specs, out_specs=out_specs, check_vma=False
    )

    def whole(trajectory, offsets, *rest):
        run = step
        return run(trajectory, offsets, *rest)

    return whole
```

```python
import functools

import jax
import jax.numpy as jnp
from jax import lax
from jax.experimental import pallas as pl
from jax.experimental.pallas import tpu as pltpu
from jax.sharding import PartitionSpec as P


BATCH = 128
COL = "col"


def layout_of(mesh):
    axis = mesh.axis_names.index(COL)
    devices = mesh.devices
    line = devices.swapaxes(0, axis).reshape(devices.shape[axis], -1)[:, 0]
    count = len(line)
    cores = 1
    if count % 2 == 0 and getattr(line[0], "coords", 0) == getattr(line[1], "coords", 0):
        cores = 2
    chips = [line[i] for i in range(0, count, cores)]
    inner = 1
    if hasattr(chips[0], "coords") and len(chips) > 1:
        start = list(chips[0].coords)
        step = [a != b for a, b in zip(start, chips[1].coords)]
        inner = 1
        while inner < len(chips) and all(
            moved or a == b for moved, a, b in zip(step, start, chips[inner].coords)
        ):
            inner += 1
        if len(chips) % inner:
            inner = 1
    outer = len(chips) // inner
    if outer == 1:
        outer, inner = inner, 1
    return outer, inner, cores


class Grid:
    def __init__(self, extents):
        self.extents = extents
        self.count = extents[0] * extents[1] * extents[2]

    def split(self, index):
        _, inner, core = self.extents
        return index // (inner * core), (index // core) % inner, index % core

    def join(self, z, y, c):
        _, inner, core = self.extents
        return (z * inner + y) * core + c

    def shift(self, dz, dy, dc):
        pairs = []
        for index in range(self.count):
            z, y, c = self.split(index)
            pairs.append((index, self.join(*self.moved((z, y, c), (dz, dy, dc)))))
        return pairs

    def moved(self, place, by):
        out = []
        for at, step, size in zip(place, by, self.extents):
            power = size & (size - 1) == 0
            out.append(at ^ step if power else (at + step) % size)
        return tuple(out)

    def back(self, place, by):
        out = []
        for at, step, size in zip(place, by, self.extents):
            power = size & (size - 1) == 0
            out.append(at ^ step if power else (at - step) % size)
        return tuple(out)

    def send(self, value, dz=0, dy=0, dc=0):
        return lax.ppermute(value, COL, self.shift(dz, dy, dc))


def halves(value):
    high = value.astype(jnp.bfloat16)
    low = (value - high.astype(jnp.float32)).astype(jnp.bfloat16)
    return high, low


def three_pass(left, right):
    width = right.shape[1]
    left_high, left_low = halves(left)
    right_high, right_low = halves(right)
    both = jnp.concatenate([right_high, right_low], axis=1)
    main = jnp.dot(left_high, both, preferred_element_type=jnp.float32)
    rest = jnp.dot(left_low, right_high, preferred_element_type=jnp.float32)
    return main[:, :width] + (main[:, width:] + rest)


def lower_part(meta_ref, lower_ref, pair, pieces, owned, bufs):
    lbuf, wbuf, lsem, wsem, stage = bufs
    outer, _, zrows = lbuf.shape
    chunks, subs = len(pieces), len(pieces[0])
    width = wbuf.shape[2] // chunks
    from_z, from_sub = outer, 2 * outer + subs

    def l_copy(k):
        cols = pl.ds(pl.multiple_of(meta_ref[from_z + k] * zrows, zrows), zrows)
        return pltpu.make_async_copy(lower_ref.at[pair, :, cols], lbuf.at[k], lsem.at[k])

    def w_copy(m, sub, k):
        rows = pl.ds(pl.multiple_of(meta_ref[from_sub + sub] * owned, owned), owned)
        return pltpu.make_async_copy(
            pieces[m][sub].at[pl.ds(k * owned, owned), :],
            wbuf.at[k, rows, pl.ds(m * width, width)],
            wsem.at[(k * subs + sub) * chunks + m],
        )

    for k in range(outer):
        if stage != "lower":
            for sub in range(subs):
                for m in range(chunks):
                    w_copy(m, sub, k).start()
        l_copy(k).start()

    def finish(total, then=None):
        def step(k, carry):
            if stage != "lower":
                for sub in range(subs):
                    for m in range(chunks):
                        w_copy(m, sub, k).wait()
            l_copy(k).wait()
            if then is not None:
                then(k)
            return carry - three_pass(lbuf[k], wbuf[k])

        return lax.fori_loop(0, outer, step, total)

    return finish


def section_kernel(sec_idx, pair, subs, meta_ref, diag_ref, lower_ref, pending_ref, *refs):
    pieces = refs[:subs] if pair is not None else ()
    refs = refs[len(pieces) :]
    outs, refs = refs[:subs], refs[subs:]
    dbuf, obuf, xbuf, dsem, osem, xsem = refs[:6]
    outer, zrows, owned = dbuf.shape
    to_sub = 2 * outer
    x_copy = pltpu.make_async_copy(pending_ref, xbuf, xsem)
    x_copy.start()
    finish = None
    if pair is not None:
        lbuf, wbuf, lsem, wsem = refs[6:]
        finish = lower_part(meta_ref, lower_ref, pair, [pieces], owned, (lbuf, wbuf, lsem, wsem, "all"))

    def d_copy(k):
        rows = pl.ds(pl.multiple_of(meta_ref[k] * zrows, zrows), zrows)
        return pltpu.make_async_copy(diag_ref.at[sec_idx, rows, :], dbuf.at[k], dsem.at[k])

    def o_copy(sub, k):
        rows = pl.ds(pl.multiple_of(k * owned, owned), owned)
        return pltpu.make_async_copy(obuf.at[sub, rows, :], outs[sub].at[rows, :], osem.at[k * subs + sub])

    if finish is None:
        for k in range(outer):
            d_copy(k).start()
    x_copy.wait()
    x = xbuf[...]
    if finish is not None:
        x = finish(x, lambda k: d_copy(k).start())
    width = x.shape[1]
    x_high, x_low = halves(x)
    both = jnp.concatenate([x_high, x_low], axis=1)

    def step(k, carry):
        d_copy(k).wait()
        for sub in range(subs):
            rows = pl.ds(pl.multiple_of(meta_ref[to_sub + sub] * owned, owned), owned)
            high, low = halves(dbuf[k, rows, :])
            main = jnp.dot(high, both, preferred_element_type=jnp.float32)
            rest = jnp.dot(low, x_high, preferred_element_type=jnp.float32)
            at = pl.ds(pl.multiple_of(k * owned, owned), owned)
            obuf[sub, at, :] = main[:, :width] + (main[:, width:] + rest)
            o_copy(sub, k).start()
        return carry

    lax.fori_loop(0, outer, step, 0)
    for k in range(outer):
        for sub in range(subs):
            o_copy(sub, k).wait()


def section_product(grid, meta, diag_inverse, lower_pairs, pending, pieces, sec_idx, pair):
    outer, inner, cores = grid.extents
    subs = inner * cores
    owned, width = pending.shape
    zrows = subs * owned
    dma = pltpu.SemaphoreType.DMA
    scratch = [
        pltpu.VMEM((outer, zrows, owned), jnp.float32),
        pltpu.VMEM((subs, outer * owned, width), jnp.float32),
        pltpu.VMEM((owned, width), jnp.float32),
        dma((outer,)),
        dma((outer * subs,)),
        dma(()),
    ]
    if pair is not None:
        scratch += [
            pltpu.VMEM((outer, owned, zrows), jnp.float32),
            pltpu.VMEM((outer, zrows, width), jnp.float32),
            dma((outer,)),
            dma((outer * subs,)),
        ]
    anywhere = pl.BlockSpec(memory_space=pl.ANY)
    return pl.pallas_call(
        functools.partial(section_kernel, sec_idx, pair, subs),
        out_shape=[jax.ShapeDtypeStruct((outer * owned, width), jnp.float32)] * subs,
        in_specs=[pl.BlockSpec(memory_space=pltpu.SMEM)] + [anywhere] * (3 + len(pieces)),
        out_specs=[anywhere] * subs,
        scratch_shapes=scratch,
    )(meta, diag_inverse, lower_pairs, pending, *pieces)


def feature_kernel(sections, sec, meta_ref, offsets_ref, ids_ref, table_ref, width_ref, path_ref, *outs):
    features = table_ref.shape[0]
    owned, lanes = outs[0].shape
    first = meta_ref[meta_ref.shape[0] - 1]
    chunks = offsets_ref.shape[0]
    lane = lax.broadcasted_iota(jnp.int32, (features, lanes), 1)
    one_lane = lax.broadcasted_iota(jnp.int32, (1, lanes), 1)
    last = path_ref.shape[1] // lanes - 1
    snaps = []
    for m in range(chunks):
        block = jnp.minimum(offsets_ref[m] // lanes, last)
        inside = offsets_ref[m] - block * lanes
        here = path_ref[:, pl.ds(pl.multiple_of(block * lanes, lanes), lanes)]
        after = path_ref[:, pl.ds(pl.multiple_of(jnp.minimum(block + 1, last) * lanes, lanes), lanes)]
        turn = (lanes - inside) % lanes
        snap = jnp.where(lane < lanes - inside, pltpu.roll(here, turn, 1), pltpu.roll(after, turn, 1))
        snaps.append((snap, jnp.sum(snap * snap, axis=0, keepdims=True)))
    for at, sec_idx in enumerate(sections):
        for group in range(owned // lanes):
            base = sec_idx * sec + first + group * lanes

            def pick(i, carry):
                centers, rates = carry
                number = ids_ref[base + i]
                block = lax.shift_right_logical(number, lanes.bit_length() - 1)
                turn = (i - number) & (lanes - 1)
                column = table_ref[:, pl.ds(pl.multiple_of(block * lanes, lanes), lanes)]
                centers = jnp.where(lane == i, pltpu.roll(column, turn, 1), centers)
                rates = jnp.where(one_lane == i, pltpu.roll(width_ref[pl.ds(block, 1), :], turn, 1), rates)
                return centers, rates

            zero = jnp.zeros((features, lanes), jnp.float32)
            centers, rates = lax.fori_loop(0, lanes, pick, (zero, zero[:1]), unroll=16)
            pad = lanes - features
            flat = jnp.concatenate([centers, jnp.broadcast_to(rates, (pad, lanes))], axis=0).T
            centers, rates = flat[:, :features], flat[:, features : features + 1]
            center_sq = jnp.sum(centers * centers, axis=1, keepdims=True)
            for m, (snap, snap_sq) in enumerate(snaps):
                cross = jnp.dot(
                    centers, snap, precision=lax.Precision.HIGHEST, preferred_element_type=jnp.float32
                )
                dist = snap_sq + center_sq - 2.0 * cross
                outs[at * chunks + m][pl.ds(group * lanes, lanes), :] = jnp.exp(-rates * dist / features)


def features_of(meta, offsets, landmark_ids, landmarks, inv_width, trajectory, owned, sec, sections):
    chunks = offsets.shape[0]
    smem = pl.BlockSpec(memory_space=pltpu.SMEM)
    vmem = pl.BlockSpec(memory_space=pltpu.VMEM)
    out = pl.pallas_call(
        functools.partial(feature_kernel, sections, sec),
        out_shape=[jax.ShapeDtypeStruct((owned, BATCH), jnp.float32)] * (chunks * len(sections)),
        in_specs=[smem, smem, smem, vmem, vmem, vmem],
        out_specs=[vmem] * (chunks * len(sections)),
        name="features",
    )(meta, offsets, landmark_ids, landmarks.T, inv_width.reshape(-1, BATCH), trajectory.T)
    return [out[at * chunks : (at + 1) * chunks] for at in range(len(sections))]


def older_kernel(pairs, subs, chunks, meta_ref, lower_ref, *refs):
    count = len(pairs)
    pendings, refs = refs[: count * chunks], refs[count * chunks :]
    pieces = [refs[m * subs : (m + 1) * subs] for m in range(chunks)]
    refs = refs[chunks * subs :]
    outs, refs = refs[: count * chunks], refs[count * chunks :]
    wbuf, wsem = refs[:2]
    bufs, sems = refs[2 : 2 + count], refs[2 + count :]
    owned, width = outs[0].shape
    finishers = []
    for at, pair in enumerate(pairs):
        bound = (bufs[at], wbuf, sems[at], wsem, "all" if at == 0 else "lower")
        finishers.append(lower_part(meta_ref, lower_ref, pair, pieces, owned, bound))
    for at in range(count):
        mine = pendings[at * chunks : (at + 1) * chunks]
        total = finishers[at](jnp.concatenate([one[...] for one in mine], axis=1))
        for m in range(chunks):
            outs[at * chunks + m][...] = total[:, m * width : (m + 1) * width]


def older_product(grid, meta, lower_pairs, pendings, pieces, pairs):
    outer, inner, cores = grid.extents
    subs, chunks = inner * cores, len(pieces)
    owned, width = pendings[0][0].shape
    zrows = subs * owned
    dma = pltpu.SemaphoreType.DMA
    anywhere = pl.BlockSpec(memory_space=pl.ANY)
    vmem = pl.BlockSpec(memory_space=pltpu.VMEM)
    count = len(pairs)
    out = pl.pallas_call(
        functools.partial(older_kernel, pairs, subs, chunks),
        out_shape=[jax.ShapeDtypeStruct((owned, width), jnp.float32)] * (count * chunks),
        in_specs=[pl.BlockSpec(memory_space=pltpu.SMEM), anywhere]
        + [vmem] * (count * chunks)
        + [anywhere] * (subs * chunks),
        out_specs=[vmem] * (count * chunks),
        scratch_shapes=[pltpu.VMEM((outer, zrows, width * chunks), jnp.float32), dma((outer * subs * chunks,))]
        + [pltpu.VMEM((outer, owned, zrows), jnp.float32)] * count
        + [dma((outer,))] * count,
        name="older",
    )(meta, lower_pairs, *[one for row in pendings for one in row], *[one for row in pieces for one in row])
    return [out[at * chunks : (at + 1) * chunks] for at in range(count)]


def body(grid, trajectory, offsets, landmarks, landmark_ids, inv_width, lower_pairs, diag_inverse):
    nsec = diag_inverse.shape[0]
    sec = diag_inverse.shape[1]
    owned = diag_inverse.shape[2]
    outer, inner, cores = grid.extents
    me = lax.axis_index(COL)
    place = grid.split(me)
    first = me * owned

    def coordinates(step):
        zs = [step(place, (dz, 0, 0))[0] for dz in range(outer)]
        subs = []
        for dc in range(cores):
            for dy in range(inner):
                _, y, c = step(place, (0, dy, dc))
                subs.append(y * cores + c)
        return zs, subs

    to_z, to_sub = coordinates(grid.moved)
    from_z, from_sub = coordinates(grid.back)
    meta = jnp.stack(to_z + from_z + to_sub + from_sub + [first]).astype(jnp.int32)

    chunks = offsets.shape[0]

    def features_in(sections):
        return features_of(
            meta, offsets, landmark_ids, landmarks, inv_width, trajectory, owned, sec, tuple(sections)
        )

    begin = features_in([0])[0]
    pending = [[begin[m]] + [None] * (nsec - 1) for m in range(chunks)]

    cut = lambda arr, i: arr[i * owned : (i + 1) * owned]

    def chunk_steps(m):
        pieces = ()
        for sec_idx in range(nsec):
            newest = sec_idx * (sec_idx - 1) // 2 + sec_idx - 1 if sec_idx else None
            yield
            parts = section_product(grid, meta, diag_inverse, lower_pairs, pending[m][sec_idx], pieces, sec_idx, newest)
            newest_pieces[m] = pieces
            own, rest = parts[:inner], parts[inner:]
            got = [
                [grid.send(rest[(dc - 1) * inner + dy], dc=dc) for dc in range(1, cores)]
                for dy in reversed(range(inner))
            ]
            yield
            plane = []
            for dy in range(1, inner):
                total = own[dy]
                for one in got[inner - 1 - dy]:
                    total = total + one
                plane.append(grid.send(total, dy=dy))
            yield
            mine = own[0]
            for one in got[-1] + plane:
                mine = mine + one
            got = [grid.send(cut(mine, dz), dz=dz) for dz in range(1, outer)]
            yield
            mine = cut(mine, 0)
            for one in got:
                mine = mine + one
            results[m][sec_idx] = mine
            if sec_idx + 1 == nsec:
                return
            got = [grid.send(mine, dz=dz) for dz in range(1, outer)]
            yield
            column = jnp.concatenate([mine] + got, axis=0)
            plane = [column] + [grid.send(column, dy=dy) for dy in range(1, inner)]
            across = [[grid.send(column, dc=dc)] for dc in range(1, cores)]
            yield
            for dc in range(1, cores):
                across[dc - 1] += [grid.send(one, dc=dc) for one in plane[1:]]
            pieces = tuple(plane + [one for row in across for one in row])

    def older_steps():
        for sections in feature_parts(nsec):
            for sec_idx, row in zip(sections, features_in(sections)):
                for m in range(chunks):
                    pending[m][sec_idx] = row[m]
            yield
        for sec_idx in range(1, nsec - 1):
            later = range(sec_idx + 1, nsec)
            pairs = [s * (s - 1) // 2 + sec_idx - 1 for s in later]
            rows = [[pending[m][s] for m in range(chunks)] for s in later]
            done = older_product(grid, meta, lower_pairs, rows, newest_pieces, pairs)
            for s, row in zip(later, done):
                for m in range(chunks):
                    pending[m][s] = row[m]
            yield

    results = [[None] * nsec for _ in range(chunks)]
    newest_pieces = [None] * chunks
    steps = [chunk_steps(m) for m in range(chunks)] + [older_steps()]
    for one in steps[:chunks]:
        next(one)
    for who, _, _ in step_order(nsec, chunks):
        next(steps[who], None)
    return jnp.concatenate([jnp.stack(one, axis=0) for one in results], axis=2)


STEPS = 6
LAGS = lambda at: 0.5 if 0 < at < 5 else 1.5


def step_order(nsec, chunks):
    keyed = []
    for sec_idx in range(nsec):
        for step in range(STEPS if sec_idx + 1 < nsec else STEPS - 2):
            at = sec_idx * STEPS + step
            lag = LAGS(at)
            keyed += [(at + m * lag, at, (m, sec_idx, step)) for m in range(chunks)]
        if sec_idx == 0:
            for part, at in zip(range(len(feature_parts(nsec))), (3.2, 4.6)):
                keyed.append((at, at, (chunks, 0, part)))
        elif sec_idx < nsec - 1:
            at = sec_idx * STEPS + 1
            keyed.append((at + 1.5 * (chunks - 1), at + 1, (chunks, sec_idx, 0)))
    return [entry for _, _, entry in sorted(keyed)]


def feature_parts(nsec):
    return [one for one in (list(range(2, nsec)), list(range(1, min(2, nsec)))) if one]


def solution(mesh):
    grid = Grid(layout_of(mesh))
    in_specs = (
        P("groups", None),
        P("groups"),
        P(),
        P(),
        P(),
        P(None, COL, None),
        P(None, None, COL),
    )
    out_specs = P(None, COL, "groups")
    step = jax.shard_map(
        functools.partial(body, grid), mesh=mesh, in_specs=in_specs, out_specs=out_specs, check_vma=False
    )

    def whole(trajectory, offsets, *rest):
        run = step
        return run(trajectory, offsets, *rest)

    return whole
```

```python
import functools

import jax
import jax.numpy as jnp
from jax import lax
from jax.experimental import pallas as pl
from jax.experimental.pallas import tpu as pltpu
from jax.sharding import PartitionSpec as P


BATCH = 128
COL = "col"


def layout_of(mesh):
    axis = mesh.axis_names.index(COL)
    devices = mesh.devices
    line = devices.swapaxes(0, axis).reshape(devices.shape[axis], -1)[:, 0]
    count = len(line)
    cores = 1
    if count % 2 == 0 and getattr(line[0], "coords", 0) == getattr(line[1], "coords", 0):
        cores = 2
    chips = [line[i] for i in range(0, count, cores)]
    inner = 1
    if hasattr(chips[0], "coords") and len(chips) > 1:
        start = list(chips[0].coords)
        step = [a != b for a, b in zip(start, chips[1].coords)]
        inner = 1
        while inner < len(chips) and all(
            moved or a == b for moved, a, b in zip(step, start, chips[inner].coords)
        ):
            inner += 1
        if len(chips) % inner:
            inner = 1
    outer = len(chips) // inner
    if outer == 1:
        outer, inner = inner, 1
    return outer, inner, cores


class Grid:
    def __init__(self, extents):
        self.extents = extents
        self.count = extents[0] * extents[1] * extents[2]

    def split(self, index):
        _, inner, core = self.extents
        return index // (inner * core), (index // core) % inner, index % core

    def join(self, z, y, c):
        _, inner, core = self.extents
        return (z * inner + y) * core + c

    def shift(self, dz, dy, dc):
        pairs = []
        for index in range(self.count):
            z, y, c = self.split(index)
            pairs.append((index, self.join(*self.moved((z, y, c), (dz, dy, dc)))))
        return pairs

    def moved(self, place, by):
        out = []
        for at, step, size in zip(place, by, self.extents):
            power = size & (size - 1) == 0
            out.append(at ^ step if power else (at + step) % size)
        return tuple(out)

    def back(self, place, by):
        out = []
        for at, step, size in zip(place, by, self.extents):
            power = size & (size - 1) == 0
            out.append(at ^ step if power else (at - step) % size)
        return tuple(out)

    def send(self, value, dz=0, dy=0, dc=0):
        return lax.ppermute(value, COL, self.shift(dz, dy, dc))


def halves(value):
    high = value.astype(jnp.bfloat16)
    low = (value - high.astype(jnp.float32)).astype(jnp.bfloat16)
    return high, low


def three_pass(left, right):
    width = right.shape[1]
    left_high, left_low = halves(left)
    right_high, right_low = halves(right)
    both = jnp.concatenate([right_high, right_low], axis=1)
    main = jnp.dot(left_high, both, preferred_element_type=jnp.float32)
    rest = jnp.dot(left_low, right_high, preferred_element_type=jnp.float32)
    return main[:, :width] + (main[:, width:] + rest)


def lower_part(meta_ref, lower_ref, pair, pieces, owned, bufs):
    lbuf, wbuf, lsem, wsem, stage = bufs
    outer, _, zrows = lbuf.shape
    chunks, subs = len(pieces), len(pieces[0])
    width = wbuf.shape[2] // chunks
    from_z, from_sub = outer, 2 * outer + subs

    def l_copy(k):
        cols = pl.ds(pl.multiple_of(meta_ref[from_z + k] * zrows, zrows), zrows)
        return pltpu.make_async_copy(lower_ref.at[pair, :, cols], lbuf.at[k], lsem.at[k])

    def w_copy(m, sub, k):
        rows = pl.ds(pl.multiple_of(meta_ref[from_sub + sub] * owned, owned), owned)
        return pltpu.make_async_copy(
            pieces[m][sub].at[pl.ds(k * owned, owned), :],
            wbuf.at[k, rows, pl.ds(m * width, width)],
            wsem.at[(k * subs + sub) * chunks + m],
        )

    for k in range(outer):
        if stage != "lower":
            for sub in range(subs):
                for m in range(chunks):
                    w_copy(m, sub, k).start()
        l_copy(k).start()

    def finish(total, then=None):
        def step(k, carry):
            if stage != "lower":
                for sub in range(subs):
                    for m in range(chunks):
                        w_copy(m, sub, k).wait()
            l_copy(k).wait()
            if then is not None:
                then(k)
            return carry - three_pass(lbuf[k], wbuf[k])

        return lax.fori_loop(0, outer, step, total)

    return finish


def section_kernel(sec_idx, pair, subs, meta_ref, diag_ref, lower_ref, pending_ref, *refs):
    pieces = refs[:subs] if pair is not None else ()
    refs = refs[len(pieces) :]
    outs, refs = refs[:subs], refs[subs:]
    dbuf, obuf, xbuf, dsem, osem, xsem = refs[:6]
    outer, zrows, owned = dbuf.shape
    to_sub = 2 * outer
    x_copy = pltpu.make_async_copy(pending_ref, xbuf, xsem)
    x_copy.start()
    finish = None
    if pair is not None:
        lbuf, wbuf, lsem, wsem = refs[6:]
        finish = lower_part(meta_ref, lower_ref, pair, [pieces], owned, (lbuf, wbuf, lsem, wsem, "all"))

    def d_copy(k):
        rows = pl.ds(pl.multiple_of(meta_ref[k] * zrows, zrows), zrows)
        return pltpu.make_async_copy(diag_ref.at[sec_idx, rows, :], dbuf.at[k], dsem.at[k])

    def o_copy(sub, k):
        rows = pl.ds(pl.multiple_of(k * owned, owned), owned)
        return pltpu.make_async_copy(obuf.at[sub, rows, :], outs[sub].at[rows, :], osem.at[k * subs + sub])

    if finish is None:
        for k in range(outer):
            d_copy(k).start()
    x_copy.wait()
    x = xbuf[...]
    if finish is not None:
        x = finish(x, lambda k: d_copy(k).start())
    width = x.shape[1]
    x_high, x_low = halves(x)
    both = jnp.concatenate([x_high, x_low], axis=1)

    def step(k, carry):
        d_copy(k).wait()
        for sub in range(subs):
            rows = pl.ds(pl.multiple_of(meta_ref[to_sub + sub] * owned, owned), owned)
            high, low = halves(dbuf[k, rows, :])
            main = jnp.dot(high, both, preferred_element_type=jnp.float32)
            rest = jnp.dot(low, x_high, preferred_element_type=jnp.float32)
            at = pl.ds(pl.multiple_of(k * owned, owned), owned)
            obuf[sub, at, :] = main[:, :width] + (main[:, width:] + rest)
            o_copy(sub, k).start()
        return carry

    lax.fori_loop(0, outer, step, 0)
    for k in range(outer):
        for sub in range(subs):
            o_copy(sub, k).wait()


def section_product(grid, meta, diag_inverse, lower_pairs, pending, pieces, sec_idx, pair):
    outer, inner, cores = grid.extents
    subs = inner * cores
    owned, width = pending.shape
    zrows = subs * owned
    dma = pltpu.SemaphoreType.DMA
    scratch = [
        pltpu.VMEM((outer, zrows, owned), jnp.float32),
        pltpu.VMEM((subs, outer * owned, width), jnp.float32),
        pltpu.VMEM((owned, width), jnp.float32),
        dma((outer,)),
        dma((outer * subs,)),
        dma(()),
    ]
    if pair is not None:
        scratch += [
            pltpu.VMEM((outer, owned, zrows), jnp.float32),
            pltpu.VMEM((outer, zrows, width), jnp.float32),
            dma((outer,)),
            dma((outer * subs,)),
        ]
    anywhere = pl.BlockSpec(memory_space=pl.ANY)
    return pl.pallas_call(
        functools.partial(section_kernel, sec_idx, pair, subs),
        out_shape=[jax.ShapeDtypeStruct((outer * owned, width), jnp.float32)] * subs,
        in_specs=[pl.BlockSpec(memory_space=pltpu.SMEM)] + [anywhere] * (3 + len(pieces)),
        out_specs=[anywhere] * subs,
        scratch_shapes=scratch,
    )(meta, diag_inverse, lower_pairs, pending, *pieces)


def feature_kernel(sections, sec, meta_ref, offsets_ref, ids_ref, table_ref, width_ref, path_ref, *outs):
    features = table_ref.shape[0]
    owned, lanes = outs[0].shape
    first = meta_ref[meta_ref.shape[0] - 1]
    chunks = offsets_ref.shape[0]
    lane = lax.broadcasted_iota(jnp.int32, (features, lanes), 1)
    one_lane = lax.broadcasted_iota(jnp.int32, (1, lanes), 1)
    last = path_ref.shape[1] // lanes - 1
    snaps = []
    for m in range(chunks):
        block = jnp.minimum(offsets_ref[m] // lanes, last)
        inside = offsets_ref[m] - block * lanes
        here = path_ref[:, pl.ds(pl.multiple_of(block * lanes, lanes), lanes)]
        after = path_ref[:, pl.ds(pl.multiple_of(jnp.minimum(block + 1, last) * lanes, lanes), lanes)]
        turn = (lanes - inside) % lanes
        snap = jnp.where(lane < lanes - inside, pltpu.roll(here, turn, 1), pltpu.roll(after, turn, 1))
        snaps.append((snap, jnp.sum(snap * snap, axis=0, keepdims=True)))
    for at, sec_idx in enumerate(sections):
        for group in range(owned // lanes):
            base = sec_idx * sec + first + group * lanes

            def pick(i, carry):
                centers, rates = carry
                number = ids_ref[base + i]
                block = lax.shift_right_logical(number, lanes.bit_length() - 1)
                turn = (i - number) & (lanes - 1)
                column = table_ref[:, pl.ds(pl.multiple_of(block * lanes, lanes), lanes)]
                centers = jnp.where(lane == i, pltpu.roll(column, turn, 1), centers)
                rates = jnp.where(one_lane == i, pltpu.roll(width_ref[pl.ds(block, 1), :], turn, 1), rates)
                return centers, rates

            zero = jnp.zeros((features, lanes), jnp.float32)
            centers, rates = lax.fori_loop(0, lanes, pick, (zero, zero[:1]), unroll=32)
            pad = lanes - features
            flat = jnp.concatenate([centers, jnp.broadcast_to(rates, (pad, lanes))], axis=0).T
            centers, rates = flat[:, :features], flat[:, features : features + 1]
            center_sq = jnp.sum(centers * centers, axis=1, keepdims=True)
            for m, (snap, snap_sq) in enumerate(snaps):
                cross = jnp.dot(
                    centers, snap, precision=lax.Precision.HIGHEST, preferred_element_type=jnp.float32
                )
                dist = snap_sq + center_sq - 2.0 * cross
                outs[at * chunks + m][pl.ds(group * lanes, lanes), :] = jnp.exp(-rates * dist / features)


def features_of(meta, offsets, landmark_ids, landmarks, inv_width, trajectory, owned, sec, sections):
    chunks = offsets.shape[0]
    smem = pl.BlockSpec(memory_space=pltpu.SMEM)
    vmem = pl.BlockSpec(memory_space=pltpu.VMEM)
    out = pl.pallas_call(
        functools.partial(feature_kernel, sections, sec),
        out_shape=[jax.ShapeDtypeStruct((owned, BATCH), jnp.float32)] * (chunks * len(sections)),
        in_specs=[smem, smem, smem, vmem, vmem, vmem],
        out_specs=[vmem] * (chunks * len(sections)),
        name="features",
    )(meta, offsets, landmark_ids, landmarks.T, inv_width.reshape(-1, BATCH), trajectory.T)
    return [out[at * chunks : (at + 1) * chunks] for at in range(len(sections))]


def older_kernel(pairs, subs, chunks, meta_ref, lower_ref, *refs):
    count = len(pairs)
    pendings, refs = refs[: count * chunks], refs[count * chunks :]
    pieces = [refs[m * subs : (m + 1) * subs] for m in range(chunks)]
    refs = refs[chunks * subs :]
    outs, refs = refs[: count * chunks], refs[count * chunks :]
    wbuf, wsem = refs[:2]
    bufs, sems = refs[2 : 2 + count], refs[2 + count :]
    owned, width = outs[0].shape
    finishers = []
    for at, pair in enumerate(pairs):
        bound = (bufs[at], wbuf, sems[at], wsem, "all" if at == 0 else "lower")
        finishers.append(lower_part(meta_ref, lower_ref, pair, pieces, owned, bound))
    for at in range(count):
        mine = pendings[at * chunks : (at + 1) * chunks]
        total = finishers[at](jnp.concatenate([one[...] for one in mine], axis=1))
        for m in range(chunks):
            outs[at * chunks + m][...] = total[:, m * width : (m + 1) * width]


def older_product(grid, meta, lower_pairs, pendings, pieces, pairs):
    outer, inner, cores = grid.extents
    subs, chunks = inner * cores, len(pieces)
    owned, width = pendings[0][0].shape
    zrows = subs * owned
    dma = pltpu.SemaphoreType.DMA
    anywhere = pl.BlockSpec(memory_space=pl.ANY)
    vmem = pl.BlockSpec(memory_space=pltpu.VMEM)
    count = len(pairs)
    out = pl.pallas_call(
        functools.partial(older_kernel, pairs, subs, chunks),
        out_shape=[jax.ShapeDtypeStruct((owned, width), jnp.float32)] * (count * chunks),
        in_specs=[pl.BlockSpec(memory_space=pltpu.SMEM), anywhere]
        + [vmem] * (count * chunks)
        + [anywhere] * (subs * chunks),
        out_specs=[vmem] * (count * chunks),
        scratch_shapes=[pltpu.VMEM((outer, zrows, width * chunks), jnp.float32), dma((outer * subs * chunks,))]
        + [pltpu.VMEM((outer, owned, zrows), jnp.float32)] * count
        + [dma((outer,))] * count,
        name="older",
    )(meta, lower_pairs, *[one for row in pendings for one in row], *[one for row in pieces for one in row])
    return [out[at * chunks : (at + 1) * chunks] for at in range(count)]


def body(grid, trajectory, offsets, landmarks, landmark_ids, inv_width, lower_pairs, diag_inverse):
    nsec = diag_inverse.shape[0]
    sec = diag_inverse.shape[1]
    owned = diag_inverse.shape[2]
    outer, inner, cores = grid.extents
    me = lax.axis_index(COL)
    place = grid.split(me)
    first = me * owned

    def coordinates(step):
        zs = [step(place, (dz, 0, 0))[0] for dz in range(outer)]
        subs = []
        for dc in range(cores):
            for dy in range(inner):
                _, y, c = step(place, (0, dy, dc))
                subs.append(y * cores + c)
        return zs, subs

    to_z, to_sub = coordinates(grid.moved)
    from_z, from_sub = coordinates(grid.back)
    meta = jnp.stack(to_z + from_z + to_sub + from_sub + [first]).astype(jnp.int32)

    chunks = offsets.shape[0]

    def features_in(sections):
        return features_of(
            meta, offsets, landmark_ids, landmarks, inv_width, trajectory, owned, sec, tuple(sections)
        )

    begin = features_in([0])[0]
    pending = [[begin[m]] + [None] * (nsec - 1) for m in range(chunks)]

    cut = lambda arr, i: arr[i * owned : (i + 1) * owned]

    def chunk_steps(m):
        pieces = ()
        for sec_idx in range(nsec):
            newest = sec_idx * (sec_idx - 1) // 2 + sec_idx - 1 if sec_idx else None
            yield
            parts = section_product(grid, meta, diag_inverse, lower_pairs, pending[m][sec_idx], pieces, sec_idx, newest)
            newest_pieces[m] = pieces
            own, rest = parts[:inner], parts[inner:]
            got = [
                [grid.send(rest[(dc - 1) * inner + dy], dc=dc) for dc in range(1, cores)]
                for dy in reversed(range(inner))
            ]
            yield
            plane = []
            for dy in range(1, inner):
                total = own[dy]
                for one in got[inner - 1 - dy]:
                    total = total + one
                plane.append(grid.send(total, dy=dy))
            yield
            mine = own[0]
            for one in got[-1] + plane:
                mine = mine + one
            got = [grid.send(cut(mine, dz), dz=dz) for dz in range(1, outer)]
            yield
            mine = cut(mine, 0)
            for one in got:
                mine = mine + one
            results[m][sec_idx] = mine
            if sec_idx + 1 == nsec:
                return
            got = [grid.send(mine, dz=dz) for dz in range(1, outer)]
            yield
            column = jnp.concatenate([mine] + got, axis=0)
            plane = [column] + [grid.send(column, dy=dy) for dy in range(1, inner)]
            across = [[grid.send(column, dc=dc)] for dc in range(1, cores)]
            yield
            for dc in range(1, cores):
                across[dc - 1] += [grid.send(one, dc=dc) for one in plane[1:]]
            pieces = tuple(plane + [one for row in across for one in row])

    def older_steps():
        for sections in feature_parts(nsec):
            for sec_idx, row in zip(sections, features_in(sections)):
                for m in range(chunks):
                    pending[m][sec_idx] = row[m]
            yield
        for sec_idx in range(1, nsec - 1):
            later = range(sec_idx + 1, nsec)
            pairs = [s * (s - 1) // 2 + sec_idx - 1 for s in later]
            rows = [[pending[m][s] for m in range(chunks)] for s in later]
            done = older_product(grid, meta, lower_pairs, rows, newest_pieces, pairs)
            for s, row in zip(later, done):
                for m in range(chunks):
                    pending[m][s] = row[m]
            yield

    results = [[None] * nsec for _ in range(chunks)]
    newest_pieces = [None] * chunks
    steps = [chunk_steps(m) for m in range(chunks)] + [older_steps()]
    for one in steps[:chunks]:
        next(one)
    for who, _, _ in step_order(nsec, chunks):
        next(steps[who], None)
    return jnp.concatenate([jnp.stack(one, axis=0) for one in results], axis=2)


STEPS = 6
FOUND = "001101021020100110101201010011010101201010110101"
LAGS = lambda at: 0.5 if 0 < at < 5 else 1.5


def step_order(nsec, chunks):
    keyed = []
    for sec_idx in range(nsec):
        for step in range(STEPS if sec_idx + 1 < nsec else STEPS - 2):
            at = sec_idx * STEPS + step
            lag = LAGS(at)
            keyed += [(at + m * lag, at, (m, sec_idx, step)) for m in range(chunks)]
        if sec_idx == 0:
            for part, at in zip(range(len(feature_parts(nsec))), (3.2, 4.6)):
                keyed.append((at, at, (chunks, 0, part)))
        elif sec_idx < nsec - 1:
            at = sec_idx * STEPS + 1
            keyed.append((at + 1.5 * (chunks - 1), at + 1, (chunks, sec_idx, 0)))
    order = [entry for _, _, entry in sorted(keyed)]
    streams = [iter(sorted(entry[1:] for entry in order if entry[0] == m)) for m in range(chunks + 1)]
    found = [int(one) for one in FOUND]
    if sorted(found) == sorted(entry[0] for entry in order):
        order = [(m, *next(streams[m])) for m in found]
    return order


def feature_parts(nsec):
    return [one for one in (list(range(2, nsec)), list(range(1, min(2, nsec)))) if one]


def solution(mesh):
    grid = Grid(layout_of(mesh))
    in_specs = (
        P("groups", None),
        P("groups"),
        P(),
        P(),
        P(),
        P(None, COL, None),
        P(None, None, COL),
    )
    out_specs = P(None, COL, "groups")
    step = jax.shard_map(
        functools.partial(body, grid), mesh=mesh, in_specs=in_specs, out_specs=out_specs, check_vma=False
    )

    def whole(trajectory, offsets, *rest):
        run = step
        return run(trajectory, offsets, *rest)

    return whole
```
